256 devices in a mesh: branch: 2 (over core), seq: 8 (over y, x_hi), rep: 16 (over z, x_lo).
Axes of the slice: x: 4 (x_hi: 2, x_lo: 2; x = x_hi * 2 + x_lo), y: 4, z: 8, core: 2. Of those that a mesh axis runs over, the one named last changes fastest.
Arguments:
- queries: bfloat16 [2, 16384, 2048], P('branch', ('rep', 'seq')), parts along dimension 1, may hold values from -64 to 64
- key_vecs: bfloat16 [2, 16384, 2048], P('branch', ('rep', 'seq')), parts along dimension 1, may hold values from -8 to 8
- value_vecs: bfloat16 [2, 16384, 2048], P('branch', ('rep', 'seq')), parts along dimension 1, may hold values from -6 to 6
- hidden_in: bfloat16 [2, 16384, 2048], P('branch', ('rep', 'seq')), parts along dimension 1, may hold values from -4 to 4
- out_proj: bfloat16 [2, 2048, 2048], P('branch', 'seq'), may hold values from -0.125 to 0.125
- couple_proj: bfloat16 [2, 2048, 2048], P('branch', 'seq'), may hold values from -0.125 to 0.125
- grad_mixed: bfloat16 [2, 16384, 2048], P('branch', ('rep', 'seq')), parts along dimension 1, may hold values from -6 to 6
Outputs:
- mixed_out: bfloat16 [2, 16384, 2048], P('branch', ('rep', 'seq')), parts along dimension 1
- grad_hidden: bfloat16 [2, 16384, 2048], P('branch', ('rep', 'seq')), parts along dimension 1
- grad_queries: bfloat16 [2, 16384, 2048], P('branch', ('rep', 'seq')), parts along dimension 1
- grad_keys: bfloat16 [2, 16384, 2048], P('branch', ('rep', 'seq')), parts along dimension 1
- grad_values: bfloat16 [2, 16384, 2048], P('branch', ('rep', 'seq')), parts along dimension 1
- grad_couple: float32 [2, 2048, 32768], P('branch', 'seq', 'rep'), parts along dimension 2
The draws below stay inside these ranges and needn't reach their ends.
There are 16 independent parts, one for each index of `rep`. The reference program is written for one: setup_inputs(seed, part) draws one part's arguments, and reference() takes and returns one part's arrays. A program takes and returns all parts, laid end to end along the dimension named above; an argument that names none is the same for every part. Nothing has to cross between parts.
All inputs are finite; a program needn't handle non-finite values.
Results may differ from the reference program's by a relative error of at most 0.015.
Values may be sent and summed in bfloat16 or wider, within the bound.
No kernel may reach another device: no remote copies, remote signals or barrier semaphores. Data moves between devices by JAX's collectives and lax.ppermute only.
A program may use at most 128 MiB of HBM per device.

```python
import math
import jax
import jax.numpy as jnp
from jax import lax

D = 2048
NH = 16
HEAD = 128
S_DEV = 128
SEQ_LEN = 1024
HE = 2048
HGROUP = 2
N_SEQ = 8


def paired_draw(key):
    shape_full = (2, SEQ_LEN, NH * HEAD)
    base_keys = jnp.clip(jax.random.normal(jax.random.fold_in(key, 101), shape_full, jnp.float32), -4.0, 4.0) * 1.5
    base_queries = jnp.clip(jax.random.normal(jax.random.fold_in(key, 102), shape_full, jnp.float32), -4.0, 4.0) * 1.5
    return (base_queries, base_keys)


def draw_queries(key, part):
    return paired_draw(key)[0].astype(jnp.bfloat16)


def draw_key_vecs(key, part):
    return paired_draw(key)[1].astype(jnp.bfloat16)


def level_of(stream_key, shape, pieces, low, high):
    gain = 1.0
    for dim, shards_of in pieces:
        heights = jax.random.uniform(jax.random.fold_in(jax.random.fold_in(stream_key, 6), dim), (shards_of,), jnp.float32, low / len(pieces), high / len(pieces))
        gain = gain * jnp.repeat(jnp.exp(heights), shape[dim] // shards_of).reshape((-1,) + (1,) * (len(shape) - 1 - dim))
    return gain


def centred(rng, extent, spread, most, shards=(), held_as=jnp.bfloat16):
    values = jax.random.normal(rng, extent, jnp.float32) * spread
    if len(shards) > 0:
        values = level_of(rng, extent, shards, -0.22, 0.18) * values
    return jnp.clip(values, min=-most, max=most).astype(held_as)


def setup_inputs(seed: int = 0, part: int = 0) -> dict:
    keys = jax.random.split(jax.random.key(seed), 8)
    part_keys = jax.random.split(jax.random.fold_in(keys[7], part), 8)
    return {
        "queries": draw_queries(jax.random.fold_in(jax.random.fold_in(keys[7], part), 71), part),
        "key_vecs": draw_key_vecs(jax.random.fold_in(jax.random.fold_in(keys[7], part), 71), part),
        "value_vecs": centred(part_keys[2], (2, SEQ_LEN, HE), 1.0, 6.0, ((0, 2), (1, 8))),
        "hidden_in": centred(part_keys[3], (2, SEQ_LEN, D), 0.5, 4.0, ((0, 2), (1, 8))),
        "out_proj": centred(keys[4], (2, HE, D), HE ** -0.5, 0.125, ((0, 2), (1, 8))),
        "couple_proj": centred(keys[5], (2, D, D), D ** -0.5, 0.125, ((0, 2), (1, 8))),
        "grad_mixed": centred(part_keys[6], (2, SEQ_LEN, D), 1.0, 6.0, ((0, 2), (1, 8))),
    }


def contract(left, right, left_dim, right_dim):
    return lax.dot_general(left, right, (((left_dim,), (right_dim,)), ((), ())), preferred_element_type=jnp.float32)

def softmax_weights(query_item, key_item, factor):
    scores = contract(query_item, key_item, 1, 1) * factor
    row_max = lax.optimization_barrier(jnp.max(scores, axis=-1, keepdims=True))
    raised = jnp.exp(scores - row_max)
    return raised / lax.optimization_barrier(jnp.sum(raised, axis=-1, keepdims=True))

def forward_item(bundle, factor):
    query_item, key_item, value_item = bundle
    weights = softmax_weights(query_item, key_item, factor)
    return contract(weights.astype(jnp.bfloat16), value_item, 1, 0).astype(jnp.bfloat16)

def backward_item(bundle, factor):
    query_item, key_item, value_item, grad_item = bundle
    weights = softmax_weights(query_item, key_item, factor)
    weights_low = weights.astype(jnp.bfloat16)
    grad_weights = contract(grad_item, value_item, 1, 1)
    row_dot = lax.optimization_barrier(jnp.sum(weights * grad_weights, axis=-1, keepdims=True))
    d_scores = (weights * (grad_weights - row_dot)).astype(jnp.bfloat16)
    grad_query = (contract(d_scores, key_item, 1, 0) * factor).astype(jnp.bfloat16)
    grad_key = (contract(d_scores, query_item, 0, 0) * factor).astype(jnp.bfloat16)
    grad_value = contract(weights_low, grad_item, 0, 0).astype(jnp.bfloat16)
    return (grad_query, grad_key, grad_value)

def to_items(whole):
    return whole.reshape(2, SEQ_LEN, NH, HEAD).transpose(0, 2, 1, 3).reshape(2 * NH, SEQ_LEN, HEAD)

def from_items(items):
    return items.reshape(2, NH, SEQ_LEN, HEAD).transpose(0, 2, 1, 3).reshape(2, SEQ_LEN, NH * HEAD)

def reference(queries, key_vecs, value_vecs, hidden_in, out_proj, couple_proj, grad_mixed):
    factor = 1.0 / math.sqrt(HEAD)
    query_items = to_items(queries)
    key_items = to_items(key_vecs)
    value_items = to_items(value_vecs)
    attended = from_items(lax.map(lambda bundle: forward_item(bundle, factor), (query_items, key_items, value_items)))
    group_width = HGROUP * HEAD
    hidden_list = []
    for branch_index in range(2):
        summed = hidden_in[branch_index].astype(jnp.float32)
        for group_index in range(NH // HGROUP):
            lower = group_index * group_width
            term = contract(attended[branch_index][:, lower:lower + group_width], out_proj[branch_index][lower:lower + group_width], 1, 0)
            summed = summed + lax.optimization_barrier(term.astype(jnp.bfloat16)).astype(jnp.float32)
        hidden_list.append(lax.optimization_barrier(summed.astype(jnp.bfloat16)))
    mixed_list = []
    back_list = []
    for branch_index in range(2):
        partner = hidden_list[1 - branch_index]
        coupled = hidden_list[branch_index].astype(jnp.float32) + contract(partner, couple_proj[branch_index], 1, 0)
        mixed_list.append(coupled.astype(jnp.bfloat16))
        back = contract(grad_mixed[branch_index], couple_proj[branch_index], 1, 1).astype(jnp.bfloat16)
        back_list.append(lax.optimization_barrier(back))
    grad_hidden_list = []
    grad_att_list = []
    couple_list = []
    for branch_index in range(2):
        grad_tok = grad_mixed[branch_index]
        grad_hid = (grad_tok.astype(jnp.float32) + back_list[1 - branch_index].astype(jnp.float32)).astype(jnp.bfloat16)
        grad_hidden_list.append(grad_hid)
        grad_att_list.append(contract(grad_hid, out_proj[branch_index], 1, 1).astype(jnp.bfloat16))
        partner_blocks = hidden_list[1 - branch_index].reshape(N_SEQ, S_DEV, D)
        grad_blocks = grad_tok.reshape(N_SEQ, S_DEV, D)

        def add_block(running, pair):
            term = contract(pair[0], pair[1], 0, 0).astype(jnp.bfloat16)
            return (running + lax.optimization_barrier(term).astype(jnp.float32), 0)
        summed, unused = lax.scan(add_block, jnp.zeros((D, D), jnp.float32), (partner_blocks, grad_blocks))
        couple_list.append(summed)
    grad_attended = jnp.stack(grad_att_list)
    grad_q, grad_k, grad_v = lax.map(lambda bundle: backward_item(bundle, factor), (query_items, key_items, value_items, to_items(grad_attended)))
    return (jnp.stack(mixed_list), jnp.stack(grad_hidden_list), from_items(grad_q), from_items(grad_k), from_items(grad_v), jnp.stack(couple_list))
```

```python
import math

import jax
import jax.numpy as jnp
from jax import lax
from jax.experimental import pallas as pl
from jax.experimental.pallas import tpu as pltpu
from jax.sharding import PartitionSpec as P

HEAD = 128
TOK = 128
CHUNK = 256
WIDE = 2 * CHUNK
FACTOR = 1.0 / math.sqrt(HEAD)
BF16 = jnp.bfloat16
F32 = jnp.float32
VMEM_LIMIT = 56 * 1024 * 1024


def seq_shift(value, mask):
    size = lax.axis_size("seq")
    return lax.ppermute(value, "seq", [(i, i ^ mask) for i in range(size)])


def branch_swap(value):
    return lax.ppermute(value, "branch", [(0, 1), (1, 0)])


def partner_rows(weight):
    seqs, reps = lax.axis_size("seq"), lax.axis_size("rep")
    pairs = [
        (s * reps + r, (s ^ 1) * reps + (r ^ 1 if reps > 1 else r))
        for s in range(seqs)
        for r in range(reps)
    ]
    return lax.ppermute(weight, ("seq", "rep"), pairs)


def dot(left, right, left_dim, right_dim):
    return lax.dot_general(
        left, right, (((left_dim,), (right_dim,)), ((), ())), preferred_element_type=F32
    )


def full(shape):
    return pl.BlockSpec(shape, lambda *_: (0,) * len(shape))


def call(body, grid, in_specs, out_specs, out_shapes, seq, args, scratch=(), name=None):
    return pl.pallas_call(
        body,
        out_shape=out_shapes,
        grid_spec=pltpu.PrefetchScalarGridSpec(
            num_scalar_prefetch=1,
            grid=grid,
            in_specs=in_specs,
            out_specs=out_specs,
            scratch_shapes=list(scratch),
        ),
        compiler_params=pltpu.CompilerParams(
            vmem_limit_bytes=VMEM_LIMIT, dimension_semantics=("arbitrary",) * len(grid)
        ),
        name=name,
    )(seq, *args)


def chunk_spec(rows, rel):
    return pl.BlockSpec((rows, CHUNK), lambda i, seq: (0, seq[0] ^ rel))


def sds(shape, dtype=BF16):
    return jax.ShapeDtypeStruct(shape, dtype)


def relative_columns(seq, arrays):
    count = len(arrays)

    def body(seq_ref, *refs):
        ins, outs = refs[: 8 * count], refs[8 * count :]
        for a in range(count):
            for rel in range(8):
                half = rel & 1
                outs[rel >> 1][a, :, half * CHUNK : (half + 1) * CHUNK] = ins[8 * a + rel][...]

    in_specs = [chunk_spec(TOK, rel) for _ in arrays for rel in range(8)]
    args = [array for array in arrays for _ in range(8)]
    return call(
        body,
        (1,),
        in_specs,
        [full((count, TOK, WIDE))] * 4,
        [sds((count, TOK, WIDE))] * 4,
        seq,
        args,
        name="relative_columns",
    )


def absolute_columns(seq, pieces, name):
    flat = [array for piece in pieces for array, _ in piece]
    count = len(pieces[0])

    def body(seq_ref, *refs):
        ins, outs = refs[: 4 * count], refs[4 * count :]
        step = pl.program_id(0)
        odd = (seq_ref[0] & 1) == 1
        for rel in range(4):

            @pl.when(step == rel)
            def _(rel=rel):
                for a in range(count):
                    low = ins[rel * count + a][:, :CHUNK]
                    high = ins[rel * count + a][:, CHUNK:]
                    outs[a][:, :CHUNK] = jnp.where(odd, high, low)
                    outs[a][:, CHUNK:] = jnp.where(odd, low, high)

    in_specs = []
    for piece in pieces:
        for array, lead in piece:
            if array.ndim == 3:
                in_specs.append(
                    pl.BlockSpec((None, TOK, WIDE), lambda i, seq, lead=lead: (lead, 0, 0))
                )
            else:
                in_specs.append(pl.BlockSpec((TOK, WIDE), lambda i, seq, lead=lead: (lead, 0)))
    out_spec = pl.BlockSpec((TOK, WIDE), lambda i, seq: (0, (seq[0] >> 1) ^ i))
    return call(
        body,
        (4,),
        in_specs,
        [out_spec] * count,
        [sds((TOK, 8 * CHUNK))] * count,
        seq,
        flat,
        name=name,
    )


def back_couple_product(seq, grads, couple):
    def body(seq_ref, g0, g1, g2, g3, w0, w1, out):
        rows = jnp.concatenate([g0[...], g1[...], g2[...], g3[...]], axis=0)
        out[:, :CHUNK] = dot(rows, w0[...], 1, 1).astype(BF16)
        out[:, CHUNK:] = dot(rows, w1[...], 1, 1).astype(BF16)

    specs = [full((TOK, 8 * CHUNK))] * 4 + [full((CHUNK, 8 * CHUNK))] * 2
    return call(
        body,
        (1,),
        specs,
        full((4 * TOK, WIDE)),
        sds((4 * TOK, WIDE)),
        seq,
        (*grads, *couple),
        name="back_couple",
    )


def grad_hidden_chunk(seq, grads, partner_back):
    def body(seq_ref, *refs):
        ins, back, out = refs[:8], refs[8], refs[9]
        for r in range(4):
            for h in range(2):
                rows = slice(r * TOK, (r + 1) * TOK)
                cols = slice(h * CHUNK, (h + 1) * CHUNK)
                total = ins[2 * r + h][...].astype(F32) + back[rows, cols].astype(F32)
                out[rows, cols] = total.astype(BF16)

    specs = [chunk_spec(TOK, h) for _ in range(4) for h in range(2)]
    args = [grad for grad in grads for _ in range(2)]
    return call(
        body,
        (1,),
        specs + [full((4 * TOK, WIDE))],
        full((4 * TOK, WIDE)),
        sds((4 * TOK, WIDE)),
        seq,
        (*args, partner_back),
        name="grad_hidden_chunk",
    )


def head_block(rows, lead, shift=0):
    return pl.BlockSpec((lead, rows, HEAD), lambda j, seq: (0, 0, (j + shift) % 4))


def proj_specs():
    return [chunk_spec(CHUNK, rel) for _ in range(2) for rel in range(8)]


def forward_partial(seq, items, partner_kv, proj):
    lead = items[0].shape[0]

    def body(seq_ref, i0, i1, i2, i3, kv, *refs):
        weights, outs, att = refs[:16], refs[16:20], refs[20]
        step = pl.program_id(0)
        query = jnp.concatenate([i0[0], i1[0], i2[0], i3[0]], axis=0)
        key = jnp.concatenate([i0[1], i1[1], i2[1], i3[1], kv[0]], axis=0)
        value = jnp.concatenate([i0[2], i1[2], i2[2], i3[2], kv[1]], axis=0)
        scores = dot(query, key, 1, 1) * FACTOR
        raised = jnp.exp(scores - jnp.max(scores, axis=-1, keepdims=True))
        total = jnp.sum(raised, axis=-1, keepdims=True)
        att[step] = (dot(raised.astype(BF16), value, 1, 0) / total).astype(BF16)

        @pl.when(step == 3)
        def _():
            first = jnp.concatenate([att[0], att[1]], axis=1)
            second = jnp.concatenate([att[2], att[3]], axis=1)
            for rel in range(8):
                dest, half = rel >> 1, rel & 1
                part = dot(first, weights[rel][...], 1, 0) + dot(
                    second, weights[8 + rel][...], 1, 0
                )
                for r in range(4):
                    rows = (r ^ dest) * TOK
                    outs[dest][rows : rows + TOK, half * CHUNK : (half + 1) * CHUNK] = part[
                        r * TOK : (r + 1) * TOK
                    ].astype(outs[dest].dtype)

    return call(
        body,
        (4,),
        [head_block(TOK, lead)] * 4 + [head_block(4 * TOK, 2, 2)] + proj_specs(),
        [full((4 * TOK, WIDE))] * 4,
        [sds((4 * TOK, WIDE), F32)] + [sds((4 * TOK, WIDE))] * 3,
        seq,
        (*items, partner_kv, *([proj[0]] * 8), *([proj[1]] * 8)),
        scratch=[pltpu.VMEM((4, 4 * TOK, HEAD), BF16)],
        name="forward_partial",
    )


def hidden_sum(seq, items, own, received):
    def body(seq_ref, i0, i1, i2, i3, own_ref, r1, r2, r3, out):
        for r, item in enumerate((i0, i1, i2, i3)):
            rows = slice(r * TOK, (r + 1) * TOK)
            total = item[...].astype(F32) + own_ref[rows]
            total = total + r1[rows].astype(F32) + r2[rows].astype(F32) + r3[rows].astype(F32)
            out[rows] = total.astype(BF16)

    last = items[0].shape[0] - 1
    item_spec = pl.BlockSpec((None, TOK, WIDE), lambda i, seq: (last, 0, 0))
    return call(
        body,
        (1,),
        [item_spec] * 4 + [full((4 * TOK, WIDE))] * 4,
        full((4 * TOK, WIDE)),
        sds((4 * TOK, WIDE)),
        seq,
        (*items, own, *received),
        name="hidden_sum",
    )


def mixed_partial(seq, partner_hidden, hidden, couple):
    def body(seq_ref, ph, hid, w0, w1, o0, o1, o2, o3):
        part = dot(ph[:, :CHUNK], w0[...], 1, 0) + dot(ph[:, CHUNK:], w1[...], 1, 0)
        first = pl.program_id(0) == 0
        odd = (seq_ref[0] & 1) == 1
        outs = (o0, o1, o2, o3)

        @pl.when(first)
        def _():
            low = hid[:, :CHUNK].astype(F32)
            high = hid[:, CHUNK:].astype(F32)
            own = jnp.concatenate([jnp.where(odd, high, low), jnp.where(odd, low, high)], axis=1)
            for r in range(4):
                rows = slice(r * TOK, (r + 1) * TOK)
                outs[r][...] = (part[rows] + own[rows]).astype(outs[r].dtype)

        @pl.when(jnp.logical_not(first))
        def _():
            for r in range(4):
                rows = slice(r * TOK, (r + 1) * TOK)
                outs[r][...] = part[rows].astype(outs[r].dtype)

    wide_cols = lambda rows: pl.BlockSpec((rows, WIDE), lambda i, seq: (0, (seq[0] >> 1) ^ i))
    return call(
        body,
        (4,),
        [full((4 * TOK, WIDE))] * 2 + [wide_cols(CHUNK)] * 2,
        [wide_cols(TOK)] * 4,
        [sds((TOK, 8 * CHUNK), F32)] + [sds((TOK, 8 * CHUNK))] * 3,
        seq,
        (partner_hidden, hidden, *couple),
        name="mixed_partial",
    )


def couple_gradient(seq, partner_hidden, grads):
    def body(seq_ref, ph, g0, g1, g2, g3, own, other):
        rows = jnp.concatenate([g0[...], g1[...], g2[...], g3[...]], axis=0)
        other[...] = dot(ph[:, CHUNK:], rows, 0, 0).astype(BF16)
        own[...] = dot(ph[:, :CHUNK], rows, 0, 0)

    cols = lambda rows: pl.BlockSpec((rows, WIDE), lambda i, seq: (0, i))
    return call(
        body,
        (4,),
        [full((4 * TOK, WIDE))] + [cols(TOK)] * 4,
        [cols(CHUNK)] * 2,
        [sds((CHUNK, 8 * CHUNK), F32), sds((CHUNK, 8 * CHUNK))],
        seq,
        (partner_hidden, *grads),
        name="couple_gradient",
    )


def backward_heads(seq, items, partner_kv, grad_chunks, proj):
    lead = items[0].shape[0]

    def body(seq_ref, i0, i1, i2, i3, kv, c0, c1, c2, c3, *refs):
        weights = refs[:16]
        dq_outs, kv_own, kv_other = refs[16:20], refs[20], refs[21]
        grad_att = refs[22]
        step = pl.program_id(0)

        @pl.when(step == 0)
        def _():
            sums = [None, None]
            for d, chunk in enumerate((c0, c1, c2, c3)):
                rows = jnp.concatenate(
                    [chunk[(r ^ d) * TOK : ((r ^ d) + 1) * TOK] for r in range(4)], axis=0
                )
                for h in range(2):
                    piece = rows[:, h * CHUNK : (h + 1) * CHUNK]
                    for part in range(2):
                        term = dot(piece, weights[8 * part + 2 * d + h][...], 1, 1)
                        sums[part] = term if sums[part] is None else sums[part] + term
            for j in range(4):
                cols = slice((j & 1) * HEAD, ((j & 1) + 1) * HEAD)
                grad_att[j] = sums[j >> 1][:, cols].astype(BF16)

        grad = grad_att[step]
        query = jnp.concatenate([i0[0], i1[0], i2[0], i3[0]], axis=0)
        key = jnp.concatenate([i0[1], i1[1], i2[1], i3[1], kv[0]], axis=0)
        value = jnp.concatenate([i0[2], i1[2], i2[2], i3[2], kv[1]], axis=0)
        scores = dot(query, key, 1, 1) * FACTOR
        raised = jnp.exp(scores - jnp.max(scores, axis=-1, keepdims=True))
        weight = raised * (1.0 / jnp.sum(raised, axis=-1, keepdims=True))
        grad_weight = dot(grad, value, 1, 1)
        row_dot = jnp.sum(weight * grad_weight, axis=-1, keepdims=True)
        d_scores = (weight * (grad_weight - row_dot)).astype(BF16)
        d_query = (dot(d_scores, key, 1, 0) * FACTOR).astype(BF16)
        d_key = (dot(d_scores, query, 0, 0) * FACTOR).astype(BF16)
        d_value = dot(weight.astype(BF16), grad, 0, 0).astype(BF16)
        for r in range(4):
            dq_outs[r][...] = d_query[r * TOK : (r + 1) * TOK]
        half = 4 * TOK
        kv_own[0] = d_key[:half]
        kv_own[1] = d_value[:half]
        kv_other[0] = d_key[half:]
        kv_other[1] = d_value[half:]

    return call(
        body,
        (4,),
        [head_block(TOK, lead)] * 4
        + [head_block(4 * TOK, 2, 2)]
        + [full((4 * TOK, WIDE))] * 4
        + proj_specs(),
        [pl.BlockSpec((TOK, HEAD), lambda j, seq: (0, j))] * 4
        + [head_block(4 * TOK, 2), head_block(4 * TOK, 2, 2)],
        [sds((TOK, WIDE))] * 4 + [sds((2, 4 * TOK, WIDE))] * 2,
        seq,
        (*items, partner_kv, *grad_chunks, *([proj[0]] * 8), *([proj[1]] * 8)),
        scratch=[pltpu.VMEM((4, 4 * TOK, HEAD), BF16)],
        name="backward_heads",
    )


def add_key_grads(seq, own, other):
    def body(seq_ref, a, b, o0, o1, o2, o3):
        for r, out in enumerate((o0, o1, o2, o3)):
            rows = slice(r * TOK, (r + 1) * TOK)
            for t in range(2):
                out[t] = (a[t, rows].astype(F32) + b[t, rows].astype(F32)).astype(BF16)

    return call(
        body,
        (1,),
        [full((2, 4 * TOK, WIDE))] * 2,
        [full((2, TOK, WIDE))] * 4,
        [sds((2, TOK, WIDE))] * 4,
        seq,
        (own, other),
        name="add_key_grads",
    )


def exchange(pieces):
    got = {r: seq_shift(pieces[r], 2 * r) for r in (2, 1, 3)}
    return [pieces[0], got[1], got[2], got[3]]


def on_device(queries, key_vecs, value_vecs, hidden_in, out_proj, couple_proj, grad_mixed):
    seq = lax.axis_index("seq").astype(jnp.int32).reshape(1)
    grad_tok = grad_mixed[0]
    grads = exchange([grad_tok] * 4)
    couple = (couple_proj[0], partner_rows(couple_proj[0]))
    pieces = relative_columns(seq, (queries[0], key_vecs[0], value_vecs[0], hidden_in[0]))
    items = exchange(pieces)
    proj = (out_proj[0], partner_rows(out_proj[0]))

    back = back_couple_product(seq, grads, couple)
    partner_back = branch_swap(back)
    chunk = grad_hidden_chunk(seq, grads, partner_back)
    chunks = exchange([chunk] * 4)

    kv_own = jnp.concatenate([item[1:3] for item in items], axis=1)
    partner_kv = seq_shift(kv_own, 1)
    partials = forward_partial(seq, items, partner_kv, proj)
    sums = exchange(partials)

    bwd = backward_heads(seq, items, partner_kv, chunks, proj)
    query_grads = exchange(bwd[:4])
    key_grads_other = seq_shift(bwd[5], 1)

    hidden = hidden_sum(seq, items, sums[0], sums[1:])
    partner_hidden = branch_swap(hidden)
    mixed_parts = exchange(mixed_partial(seq, partner_hidden, hidden, couple))
    couple_own, couple_other = couple_gradient(seq, partner_hidden, grads)
    couple_got = seq_shift(couple_other, 1)

    key_grads = exchange(add_key_grads(seq, bwd[4], key_grads_other))

    (grad_hid,) = absolute_columns(
        seq, [[(chunks[r], r)] for r in range(4)], "grad_hidden_columns"
    )
    mixed = mixed_parts[0]
    for part in mixed_parts[1:]:
        mixed = mixed + part.astype(F32)
    grad_cpl = couple_own + couple_got.astype(F32)
    grad_q, grad_k, grad_v = absolute_columns(
        seq,
        [[(query_grads[r], 0), (key_grads[r], 0), (key_grads[r], 1)] for r in range(4)],
        "grad_columns",
    )
    return (
        mixed.astype(BF16)[None],
        grad_hid[None],
        grad_q[None],
        grad_k[None],
        grad_v[None],
        grad_cpl[None],
    )


def solution(mesh):
    return jax.shard_map(
        on_device,
        mesh=mesh,
        in_specs=(
            P("branch", ("rep", "seq"), None),
            P("branch", ("rep", "seq"), None),
            P("branch", ("rep", "seq"), None),
            P("branch", ("rep", "seq"), None),
            P("branch", "seq", None),
            P("branch", "seq", None),
            P("branch", ("rep", "seq"), None),
        ),
        out_specs=(
            P("branch", ("rep", "seq"), None),
            P("branch", ("rep", "seq"), None),
            P("branch", ("rep", "seq"), None),
            P("branch", ("rep", "seq"), None),
            P("branch", ("rep", "seq"), None),
            P("branch", "seq", "rep"),
        ),
        check_vma=False,
    )
```

```python
import math

import jax
import jax.numpy as jnp
from jax import lax
from jax.experimental import pallas as pl
from jax.experimental.pallas import tpu as pltpu
from jax.sharding import PartitionSpec as P


HEAD = 128
TOK = 128
CHUNK = 256
WIDE = 2 * CHUNK
FACTOR = 1.0 / math.sqrt(HEAD)
BF16 = jnp.bfloat16
F32 = jnp.float32
VMEM_LIMIT = 56 * 1024 * 1024


def seq_shift(value, mask):
    size = lax.axis_size("seq")
    return lax.ppermute(value, "seq", [(i, i ^ mask) for i in range(size)])


def branch_swap(value):
    return lax.ppermute(value, "branch", [(0, 1), (1, 0)])


def partner_rows(weight):
    seqs, reps = lax.axis_size("seq"), lax.axis_size("rep")
    pairs = [
        (s * reps + r, (s ^ 1) * reps + (r ^ 1 if reps > 1 else r))
        for s in range(seqs)
        for r in range(reps)
    ]
    return lax.ppermute(weight, ("seq", "rep"), pairs)


def dot(left, right, left_dim, right_dim):
    return lax.dot_general(
        left, right, (((left_dim,), (right_dim,)), ((), ())), preferred_element_type=F32
    )


def full(shape):
    return pl.BlockSpec(shape, lambda *_: (0,) * len(shape))


def call(body, grid, in_specs, out_specs, out_shapes, seq, args, scratch=()):
    return pl.pallas_call(
        body,
        out_shape=out_shapes,
        grid_spec=pltpu.PrefetchScalarGridSpec(
            num_scalar_prefetch=1,
            grid=grid,
            in_specs=in_specs,
            out_specs=out_specs,
            scratch_shapes=list(scratch),
        ),
        compiler_params=pltpu.CompilerParams(
            vmem_limit_bytes=VMEM_LIMIT, dimension_semantics=("arbitrary",) * len(grid)
        ),
    )(seq, *args)


def chunk_spec(rows, rel):
    return pl.BlockSpec((rows, CHUNK), lambda i, seq: (0, seq[0] ^ rel))


def sds(shape, dtype=BF16):
    return jax.ShapeDtypeStruct(shape, dtype)


def relative_columns(seq, arrays):
    count = len(arrays)

    def body(seq_ref, *refs):
        ins, outs = refs[: 8 * count], refs[8 * count :]
        for a in range(count):
            for rel in range(8):
                half = rel & 1
                outs[rel >> 1][a, :, half * CHUNK : (half + 1) * CHUNK] = ins[8 * a + rel][...]

    in_specs = [chunk_spec(TOK, rel) for _ in arrays for rel in range(8)]
    args = [array for array in arrays for _ in range(8)]
    return call(
        body,
        (1,),
        in_specs,
        [full((count, TOK, WIDE))] * 4,
        [sds((count, TOK, WIDE))] * 4,
        seq,
        args,
    )


def absolute_columns(seq, halves):
    flat = [block for piece in halves for pair in piece for block in pair]
    count = len(halves[0])

    def body(seq_ref, *refs):
        ins, outs = refs[: 8 * count], refs[8 * count :]
        step = pl.program_id(0)
        odd = (seq_ref[0] & 1) == 1
        for rel in range(4):

            @pl.when(step == rel)
            def _(rel=rel):
                for a in range(count):
                    low = ins[2 * (rel * count + a)][...]
                    high = ins[2 * (rel * count + a) + 1][...]
                    outs[a][:, :CHUNK] = jnp.where(odd, high, low)
                    outs[a][:, CHUNK:] = jnp.where(odd, low, high)

    out_spec = pl.BlockSpec((TOK, WIDE), lambda i, seq: (0, (seq[0] >> 1) ^ i))
    return call(
        body,
        (4,),
        [spec for _, spec in flat],
        [out_spec] * count,
        [sds((TOK, 8 * CHUNK))] * count,
        seq,
        [array for array, _ in flat],
    )


def back_couple_product(seq, grads, couple):
    def body(seq_ref, g0, g1, g2, g3, w0, w1, out):
        rows = jnp.concatenate([g0[...], g1[...], g2[...], g3[...]], axis=0)
        out[:, :CHUNK] = dot(rows, w0[...], 1, 1).astype(BF16)
        out[:, CHUNK:] = dot(rows, w1[...], 1, 1).astype(BF16)

    specs = [full((TOK, 8 * CHUNK))] * 4 + [full((CHUNK, 8 * CHUNK))] * 2
    return call(
        body,
        (1,),
        specs,
        full((4 * TOK, WIDE)),
        sds((4 * TOK, WIDE)),
        seq,
        (*grads, *couple),
    )


def grad_hidden_chunk(seq, grads, partner_back):
    def body(seq_ref, *refs):
        ins, back, out = refs[:8], refs[8], refs[9]
        for r in range(4):
            for h in range(2):
                rows = slice(r * TOK, (r + 1) * TOK)
                cols = slice(h * CHUNK, (h + 1) * CHUNK)
                total = ins[2 * r + h][...].astype(F32) + back[rows, cols].astype(F32)
                out[rows, cols] = total.astype(BF16)

    specs = [chunk_spec(TOK, h) for _ in range(4) for h in range(2)]
    args = [grad for grad in grads for _ in range(2)]
    return call(
        body,
        (1,),
        specs + [full((4 * TOK, WIDE))],
        full((4 * TOK, WIDE)),
        sds((4 * TOK, WIDE)),
        seq,
        (*args, partner_back),
    )


def proj_specs():
    return [chunk_spec(CHUNK, rel) for _ in range(2) for rel in range(8)]


def head_specs(first):
    query = pl.BlockSpec((None, TOK, HEAD), lambda j, seq: (0, 0, j + first))
    pair = pl.BlockSpec((2, TOK, HEAD), lambda j, seq: (0, 0, j + first))
    other = pl.BlockSpec((2, TOK, HEAD), lambda j, seq: (0, 0, (j + first + 2) % 4))
    return [query] * 4 + [pair] * 4 + [other] * 4


def head_values(refs):
    query = jnp.concatenate([ref[...] for ref in refs[:4]], axis=0)
    key = jnp.concatenate([ref[0] for ref in refs[4:12]], axis=0)
    value = jnp.concatenate([ref[1] for ref in refs[4:12]], axis=0)
    return query, key, value


def raised_scores(query, key):
    scores = dot(query, key, 1, 1)
    base = FACTOR * math.log2(math.e)
    return jnp.exp2(scores * base - jnp.max(scores, axis=-1, keepdims=True) * base)


def attend(seq, heads):
    def body(seq_ref, *refs):
        query, key, value = head_values(refs)
        raised = raised_scores(query, key)
        total = jnp.sum(raised, axis=-1, keepdims=True)
        refs[12][...] = (dot(raised.astype(BF16), value, 1, 0) / total).astype(BF16)

    return call(
        body,
        (4,),
        head_specs(0),
        pl.BlockSpec((4 * TOK, HEAD), lambda j, seq: (0, j)),
        sds((4 * TOK, WIDE)),
        seq,
        heads,
    )


def output_partial(seq, attended, proj):
    def body(seq_ref, att, *refs):
        weights, outs = refs[:16], refs[16:]
        first, second = att[:, :CHUNK], att[:, CHUNK:]
        for rel in range(8):
            dest, half = rel >> 1, rel & 1
            part = dot(first, weights[rel][...], 1, 0) + dot(second, weights[8 + rel][...], 1, 0)
            for r in range(4):
                rows = (r ^ dest) * TOK
                outs[dest][rows : rows + TOK, half * CHUNK : (half + 1) * CHUNK] = part[
                    r * TOK : (r + 1) * TOK
                ].astype(outs[dest].dtype)

    return call(
        body,
        (1,),
        [full((4 * TOK, WIDE))] + proj_specs(),
        [full((4 * TOK, WIDE))] * 4,
        [sds((4 * TOK, WIDE), F32)] + [sds((4 * TOK, WIDE))] * 3,
        seq,
        (attended, *([proj[0]] * 8), *([proj[1]] * 8)),
    )


def hidden_sum(seq, items, own, received):
    def body(seq_ref, i0, i1, i2, i3, own_ref, r1, r2, r3, out):
        for r, item in enumerate((i0, i1, i2, i3)):
            rows = slice(r * TOK, (r + 1) * TOK)
            total = item[...].astype(F32) + own_ref[rows]
            total = total + r1[rows].astype(F32) + r2[rows].astype(F32) + r3[rows].astype(F32)
            out[rows] = total.astype(BF16)

    item_spec = pl.BlockSpec((None, TOK, WIDE), lambda i, seq: (0, 0, 0))
    return call(
        body,
        (1,),
        [item_spec] * 4 + [full((4 * TOK, WIDE))] * 4,
        full((4 * TOK, WIDE)),
        sds((4 * TOK, WIDE)),
        seq,
        (*items, own, *received),
    )


def mixed_partial(seq, partner_hidden, hidden, couple):
    def body(seq_ref, ph, hid, w0, w1, o0, o1, o2, o3):
        part = dot(ph[:, :CHUNK], w0[...], 1, 0) + dot(ph[:, CHUNK:], w1[...], 1, 0)
        first = pl.program_id(0) == 0
        odd = (seq_ref[0] & 1) == 1
        outs = (o0, o1, o2, o3)

        @pl.when(first)
        def _():
            low = hid[:, :CHUNK].astype(F32)
            high = hid[:, CHUNK:].astype(F32)
            own = jnp.concatenate([jnp.where(odd, high, low), jnp.where(odd, low, high)], axis=1)
            for r in range(4):
                rows = slice(r * TOK, (r + 1) * TOK)
                outs[r][...] = (part[rows] + own[rows]).astype(outs[r].dtype)

        @pl.when(jnp.logical_not(first))
        def _():
            for r in range(4):
                rows = slice(r * TOK, (r + 1) * TOK)
                outs[r][...] = part[rows].astype(outs[r].dtype)

    wide_cols = lambda rows: pl.BlockSpec((rows, WIDE), lambda i, seq: (0, (seq[0] >> 1) ^ i))
    return call(
        body,
        (4,),
        [full((4 * TOK, WIDE))] * 2 + [wide_cols(CHUNK)] * 2,
        [wide_cols(TOK)] * 4,
        [sds((TOK, 8 * CHUNK), F32)] + [sds((TOK, 8 * CHUNK))] * 3,
        seq,
        (partner_hidden, hidden, *couple),
    )


def couple_gradient(seq, partner_hidden, grads):
    def body(seq_ref, ph, g0, g1, g2, g3, own, other):
        rows = jnp.concatenate([g0[...], g1[...], g2[...], g3[...]], axis=0)
        other[...] = dot(ph[:, CHUNK:], rows, 0, 0).astype(BF16)
        own[...] = dot(ph[:, :CHUNK], rows, 0, 0)

    cols = lambda rows: pl.BlockSpec((rows, WIDE), lambda i, seq: (0, i))
    return call(
        body,
        (4,),
        [full((4 * TOK, WIDE))] + [cols(TOK)] * 4,
        [cols(CHUNK)] * 2,
        [sds((CHUNK, 8 * CHUNK), F32), sds((CHUNK, 8 * CHUNK))],
        seq,
        (partner_hidden, *grads),
    )


def backward_half(seq, heads, grad_chunks, proj_rows, half):
    def body(seq_ref, *refs):
        chunks, weights = refs[12:16], refs[16:24]
        dq_out, kv_own, kv_other, grad_att = refs[24:28]
        step = pl.program_id(0)

        @pl.when(step == 0)
        def _():
            total = None
            for d, chunk in enumerate(chunks):
                rows = jnp.concatenate(
                    [chunk[(r ^ d) * TOK : ((r ^ d) + 1) * TOK] for r in range(4)], axis=0
                )
                for h in range(2):
                    piece = rows[:, h * CHUNK : (h + 1) * CHUNK]
                    term = dot(piece, weights[2 * d + h][...], 1, 1)
                    total = term if total is None else total + term
            grad_att[0] = total[:, :HEAD].astype(BF16)
            grad_att[1] = total[:, HEAD:].astype(BF16)

        grad = grad_att[step]
        query, key, value = head_values(refs)
        raised = raised_scores(query, key)
        weight = raised * (1.0 / jnp.sum(raised, axis=-1, keepdims=True))
        grad_weight = dot(grad, value, 1, 1)
        row_dot = jnp.sum(weight * grad_weight, axis=-1, keepdims=True)
        d_scores = (weight * (grad_weight - row_dot)).astype(BF16)
        dq_out[...] = (dot(d_scores, key, 1, 0) * FACTOR).astype(BF16)
        d_key = (dot(d_scores, query, 0, 0) * FACTOR).astype(BF16)
        d_value = dot(weight.astype(BF16), grad, 0, 0).astype(BF16)
        rows = 4 * TOK
        kv_own[0] = d_key[:rows]
        kv_own[1] = d_value[:rows]
        kv_other[0] = d_key[rows:]
        kv_other[1] = d_value[rows:]

    pair = pl.BlockSpec((2, 4 * TOK, HEAD), lambda j, seq: (0, 0, j))
    return call(
        body,
        (2,),
        head_specs(2 * half)
        + [full((4 * TOK, WIDE))] * 4
        + [chunk_spec(CHUNK, rel) for rel in range(8)],
        [pl.BlockSpec((4 * TOK, HEAD), lambda j, seq: (0, j)), pair, pair],
        [sds((4 * TOK, CHUNK))] + [sds((2, 4 * TOK, CHUNK))] * 2,
        seq,
        (*heads, *grad_chunks, *([proj_rows] * 8)),
        scratch=[pltpu.VMEM((2, 4 * TOK, HEAD), BF16)],
    )


def add_key_grads(seq, own, other, query_grads):
    count = 2 + len(query_grads)

    def body(seq_ref, a, b, *refs):
        ins, outs = refs[: count - 2], refs[count - 2 :]
        for r, out in enumerate(outs):
            rows = slice(r * TOK, (r + 1) * TOK)
            for t in range(2):
                out[t] = (a[t, rows].astype(F32) + b[t, rows].astype(F32)).astype(BF16)
            for t, ref in enumerate(ins):
                out[2 + t] = ref[rows]

    return call(
        body,
        (1,),
        [full((2, 4 * TOK, CHUNK))] * 2 + [full((4 * TOK, CHUNK))] * (count - 2),
        [full((count, TOK, CHUNK))] * 4,
        [sds((count, TOK, CHUNK))] * 4,
        seq,
        (own, other, *query_grads),
    )


def exchange(pieces):
    got = [pieces[0], None, None, None]
    for r in (2, 1, 3):
        got[r] = seq_shift(pieces[r], 2 * r)
    return got


def half_block(array, lead):
    return (array, pl.BlockSpec((None, TOK, CHUNK), lambda i, seq: (lead, 0, 0)))


def steps(queries, key_vecs, value_vecs, hidden_in, out_proj, couple_proj, grad_mixed):
    seq = lax.axis_index("seq").astype(jnp.int32).reshape(1)
    pairs = relative_columns(seq, (key_vecs[0], value_vecs[0]))
    pairs = exchange(pairs)
    others = [seq_shift(pairs[r], 1) for r in range(4)]
    items = exchange(relative_columns(seq, (queries[0],)))
    grads = exchange([grad_mixed[0]] * 4)
    couple = (couple_proj[0], partner_rows(couple_proj[0]))
    inputs = exchange(relative_columns(seq, (hidden_in[0],)))
    late_proj, _ = lax.optimization_barrier((out_proj[0], couple[1]))
    proj = (out_proj[0], partner_rows(late_proj))
    heads = (*items, *pairs, *others)

    back = back_couple_product(seq, grads, couple)
    partner_back = branch_swap(back)
    chunk = grad_hidden_chunk(seq, grads, partner_back)
    chunks = exchange([chunk] * 4)

    sums = exchange(output_partial(seq, attend(seq, heads), proj))

    first = backward_half(seq, heads, chunks, proj[0], 0)
    got_high = seq_shift(first[2], 1)
    second = backward_half(seq, heads, chunks, proj[1], 1)
    got_low = seq_shift(second[2], 1)

    hidden = hidden_sum(seq, inputs, sums[0], sums[1:])
    partner_hidden = branch_swap(hidden)
    mixed_parts = exchange(mixed_partial(seq, partner_hidden, hidden, couple))
    couple_own, couple_other = couple_gradient(seq, partner_hidden, grads)
    couple_got = seq_shift(couple_other, 1)

    high = add_key_grads(seq, second[1], got_high, (first[0], second[0]))
    high = exchange(high)
    low = exchange(add_key_grads(seq, first[1], got_low, ()))

    def chunk_half(r, h):
        return (chunks[r], pl.BlockSpec((TOK, CHUNK), lambda i, seq: (r, h)))

    (grad_hid,) = absolute_columns(
        seq, [[(chunk_half(r, 0), chunk_half(r, 1))] for r in range(4)]
    )
    mixed = mixed_parts[0]
    for part in mixed_parts[1:]:
        mixed = mixed + part.astype(F32)
    grad_cpl = couple_own + couple_got.astype(F32)
    grad_q, grad_k, grad_v = absolute_columns(
        seq,
        [
            [
                (half_block(high[r], 2), half_block(high[r], 3)),
                (half_block(low[r], 0), half_block(high[r], 0)),
                (half_block(low[r], 1), half_block(high[r], 1)),
            ]
            for r in range(4)
        ],
    )
    return (
        mixed.astype(BF16)[None],
        grad_hid[None],
        grad_q[None],
        grad_k[None],
        grad_v[None],
        grad_cpl[None],
    )


def solution(mesh):
    return jax.shard_map(
        steps,
        mesh=mesh,
        in_specs=(
            P("branch", ("rep", "seq"), None),
            P("branch", ("rep", "seq"), None),
            P("branch", ("rep", "seq"), None),
            P("branch", ("rep", "seq"), None),
            P("branch", "seq", None),
            P("branch", "seq", None),
            P("branch", ("rep", "seq"), None),
        ),
        out_specs=(
            P("branch", ("rep", "seq"), None),
            P("branch", ("rep", "seq"), None),
            P("branch", ("rep", "seq"), None),
            P("branch", ("rep", "seq"), None),
            P("branch", ("rep", "seq"), None),
            P("branch", "seq", "rep"),
        ),
        check_vma=False,
    )
```

```python
import math

import jax
import jax.numpy as jnp
from jax import lax
from jax.experimental import pallas as pl
from jax.experimental.pallas import tpu as pltpu
from jax.sharding import PartitionSpec as P


HEAD = 128
TOK = 128
CHUNK = 256
WIDE = 2 * CHUNK
FACTOR = 1.0 / math.sqrt(HEAD)
BF16 = jnp.bfloat16
F32 = jnp.float32
VMEM_LIMIT = 56 * 1024 * 1024


def seq_shift(value, mask):
    size = lax.axis_size("seq")
    return lax.ppermute(value, "seq", [(i, i ^ mask) for i in range(size)])


def branch_swap(value):
    return lax.ppermute(value, "branch", [(0, 1), (1, 0)])


def rep_shift(value, mask):
    seqs, reps = lax.axis_size("seq"), lax.axis_size("rep")
    pairs = [
        (s * reps + r, (s ^ mask) * reps + (r ^ 1)) for s in range(seqs) for r in range(reps)
    ]
    return lax.ppermute(value, ("seq", "rep"), pairs)


def half_rows(weight, odd_rep):
    return lax.dynamic_slice(weight, (HEAD * (1 - odd_rep), 0), (HEAD, weight.shape[1]))


def dot(left, right, left_dim, right_dim):
    return lax.dot_general(
        left, right, (((left_dim,), (right_dim,)), ((), ())), preferred_element_type=F32
    )


def full(shape):
    return pl.BlockSpec(shape, lambda *_: (0,) * len(shape))


def call(body, grid, in_specs, out_specs, out_shapes, seq, args, scratch=()):
    return pl.pallas_call(
        body,
        out_shape=out_shapes,
        grid_spec=pltpu.PrefetchScalarGridSpec(
            num_scalar_prefetch=1,
            grid=grid,
            in_specs=in_specs,
            out_specs=out_specs,
            scratch_shapes=list(scratch),
        ),
        compiler_params=pltpu.CompilerParams(
            vmem_limit_bytes=VMEM_LIMIT, dimension_semantics=("arbitrary",) * len(grid)
        ),
    )(seq, *args)


def chunk_spec(rows, rel):
    return pl.BlockSpec((rows, CHUNK), lambda i, seq: (0, seq[0] ^ rel))


def sds(shape, dtype=BF16):
    return jax.ShapeDtypeStruct(shape, dtype)


def relative_columns(seq, arrays):
    count = len(arrays)

    def body(seq_ref, *refs):
        ins, outs = refs[: 8 * count], refs[8 * count :]
        for a in range(count):
            for rel in range(8):
                half = rel & 1
                outs[rel >> 1][a, :, half * CHUNK : (half + 1) * CHUNK] = ins[8 * a + rel][...]

    in_specs = [chunk_spec(TOK, rel) for _ in arrays for rel in range(8)]
    args = [array for array in arrays for _ in range(8)]
    return call(
        body,
        (1,),
        in_specs,
        [full((count, TOK, WIDE))] * 4,
        [sds((count, TOK, WIDE))] * 4,
        seq,
        args,
    )


def absolute_columns(seq, halves):
    flat = [block for piece in halves for pair in piece for block in pair]
    count = len(halves[0])

    def body(seq_ref, *refs):
        ins, outs = refs[: 8 * count], refs[8 * count :]
        step = pl.program_id(0)
        odd = (seq_ref[0] & 1) == 1
        for rel in range(4):

            @pl.when(step == rel)
            def _(rel=rel):
                for a in range(count):
                    low = ins[2 * (rel * count + a)][...]
                    high = ins[2 * (rel * count + a) + 1][...]
                    outs[a][:, :CHUNK] = jnp.where(odd, high, low)
                    outs[a][:, CHUNK:] = jnp.where(odd, low, high)

    out_spec = pl.BlockSpec((TOK, WIDE), lambda i, seq: (0, (seq[0] >> 1) ^ i))
    return call(
        body,
        (4,),
        [spec for _, spec in flat],
        [out_spec] * count,
        [sds((TOK, 8 * CHUNK))] * count,
        seq,
        [array for array, _ in flat],
    )


def split_specs():
    return [
        pl.BlockSpec((4 * TOK, CHUNK), lambda i, seq: (0, 0)),
        pl.BlockSpec((4 * TOK, HEAD), lambda i, seq: (0, 2 + seq[1])),
        pl.BlockSpec((4 * TOK, HEAD), lambda i, seq: (0, 3 - seq[1])),
    ]


def back_couple_product(seq, grads, couple):
    def body(seq_ref, g0, g1, g2, g3, w0, w1, w2, out):
        rows = jnp.concatenate([g0[...], g1[...], g2[...], g3[...]], axis=0)
        out[:, :CHUNK] = dot(rows, w0[...], 1, 1).astype(BF16)
        out[:, CHUNK:] = dot(rows, jnp.concatenate([w1[...], w2[...]], axis=0), 1, 1).astype(BF16)

    specs = [full((TOK, 8 * CHUNK))] * 4 + [full((CHUNK, 8 * CHUNK))]
    specs = specs + [full((HEAD, 8 * CHUNK))] * 2
    return call(
        body, (1,), specs, full((4 * TOK, WIDE)), sds((4 * TOK, WIDE)), seq, (*grads, *couple)
    )


def grad_hidden_chunk(seq, grads, partner_back):
    def body(seq_ref, *refs):
        ins, backs, out = refs[:8], refs[8:11], refs[11]
        for r in range(4):
            rows = slice(r * TOK, (r + 1) * TOK)
            low = ins[2 * r][...].astype(F32) + backs[0][rows].astype(F32)
            out[rows, :CHUNK] = low.astype(BF16)
            for p in range(2):
                cols = slice(p * HEAD, (p + 1) * HEAD)
                high = ins[2 * r + 1][:, cols].astype(F32) + backs[1 + p][rows].astype(F32)
                out[rows, CHUNK + p * HEAD : CHUNK + (p + 1) * HEAD] = high.astype(BF16)

    specs = [chunk_spec(TOK, h) for _ in range(4) for h in range(2)]
    args = [grad for grad in grads for _ in range(2)]
    return call(
        body,
        (1,),
        specs + split_specs(),
        full((4 * TOK, WIDE)),
        sds((4 * TOK, WIDE)),
        seq,
        (*args, *([partner_back] * 3)),
    )


def head_at(j, seq):
    return j ^ (seq[1] & (j >> 1))


def head_specs(first):
    at = lambda j, seq: (0, 0, head_at(j + first, seq))
    swapped = lambda j, seq: (0, 0, head_at(j + first, seq) ^ 2)
    query = pl.BlockSpec((None, TOK, HEAD), at)
    pair = pl.BlockSpec((2, TOK, HEAD), at)
    other = pl.BlockSpec((2, TOK, HEAD), swapped)
    return [query] * 4 + [pair] * 4 + [other] * 4


def head_values(refs):
    query = jnp.concatenate([ref[...] for ref in refs[:4]], axis=0)
    key = jnp.concatenate([ref[0] for ref in refs[4:12]], axis=0)
    value = jnp.concatenate([ref[1] for ref in refs[4:12]], axis=0)
    return query, key, value


def raised_scores(query, key):
    scores = dot(query, key, 1, 1)
    base = FACTOR * math.log2(math.e)
    return jnp.exp2(scores * base - jnp.max(scores, axis=-1, keepdims=True) * base)


def attend(seq, heads):
    def body(seq_ref, *refs):
        query, key, value = head_values(refs)
        raised = raised_scores(query, key)
        total = jnp.sum(raised, axis=-1, keepdims=True)
        refs[12][...] = (dot(raised.astype(BF16), value, 1, 0) / total).astype(BF16)

    return call(
        body,
        (4,),
        head_specs(0),
        pl.BlockSpec((4 * TOK, HEAD), lambda j, seq: (0, j)),
        sds((4 * TOK, WIDE)),
        seq,
        heads,
    )


def output_partial(seq, attended, proj):
    def body(seq_ref, att, *refs):
        weights, outs = refs[:24], refs[24:]
        first, second = att[:, :CHUNK], att[:, CHUNK:]
        for rel in range(8):
            dest, half = rel >> 1, rel & 1
            held = jnp.concatenate([weights[8 + rel][...], weights[16 + rel][...]], axis=0)
            part = dot(first, weights[rel][...], 1, 0) + dot(second, held, 1, 0)
            for r in range(4):
                rows = (r ^ dest) * TOK
                outs[dest][rows : rows + TOK, half * CHUNK : (half + 1) * CHUNK] = part[
                    r * TOK : (r + 1) * TOK
                ].astype(outs[dest].dtype)

    return call(
        body,
        (1,),
        [full((4 * TOK, WIDE))]
        + [chunk_spec(rows, rel) for rows in (CHUNK, HEAD, HEAD) for rel in range(8)],
        [full((4 * TOK, WIDE))] * 4,
        [sds((4 * TOK, WIDE), F32)] + [sds((4 * TOK, WIDE))] * 3,
        seq,
        (attended, *[weight for weight in proj for _ in range(8)]),
    )


def hidden_sum(seq, items, own, received):
    def body(seq_ref, i0, i1, i2, i3, own_ref, r1, r2, r3, out):
        for r, item in enumerate((i0, i1, i2, i3)):
            rows = slice(r * TOK, (r + 1) * TOK)
            total = item[...].astype(F32) + own_ref[rows]
            total = total + r1[rows].astype(F32) + r2[rows].astype(F32) + r3[rows].astype(F32)
            out[rows] = total.astype(BF16)

    item_spec = pl.BlockSpec((None, TOK, WIDE), lambda i, seq: (0, 0, 0))
    return call(
        body,
        (1,),
        [item_spec] * 4 + [full((4 * TOK, WIDE))] * 4,
        full((4 * TOK, WIDE)),
        sds((4 * TOK, WIDE)),
        seq,
        (*items, own, *received),
    )


def mixed_partial(seq, partner_hidden, hidden, couple):
    def body(seq_ref, p0, p1, p2, hid, w0, w1, w2, o0, o1, o2, o3):
        held = jnp.concatenate([w1[...], w2[...]], axis=0)
        part = dot(p0[...], w0[...], 1, 0)
        part = part + dot(jnp.concatenate([p1[...], p2[...]], axis=1), held, 1, 0)
        first = pl.program_id(0) == 0
        odd = (seq_ref[0] & 1) == 1
        outs = (o0, o1, o2, o3)

        @pl.when(first)
        def _():
            low = hid[:, :CHUNK].astype(F32)
            high = hid[:, CHUNK:].astype(F32)
            own = jnp.concatenate([jnp.where(odd, high, low), jnp.where(odd, low, high)], axis=1)
            for r in range(4):
                rows = slice(r * TOK, (r + 1) * TOK)
                outs[r][...] = (part[rows] + own[rows]).astype(outs[r].dtype)

        @pl.when(jnp.logical_not(first))
        def _():
            for r in range(4):
                rows = slice(r * TOK, (r + 1) * TOK)
                outs[r][...] = part[rows].astype(outs[r].dtype)

    wide_cols = lambda rows: pl.BlockSpec((rows, WIDE), lambda i, seq: (0, (seq[0] >> 1) ^ i))
    return call(
        body,
        (4,),
        split_specs()
        + [full((4 * TOK, WIDE))]
        + [wide_cols(rows) for rows in (CHUNK, HEAD, HEAD)],
        [wide_cols(TOK)] * 4,
        [sds((TOK, 8 * CHUNK), F32)] + [sds((TOK, 8 * CHUNK))] * 3,
        seq,
        (*([partner_hidden] * 3), hidden, *couple),
    )


def couple_gradient(seq, partner_hidden, grads):
    def body(seq_ref, ph, g0, g1, g2, g3, own, other):
        rows = jnp.concatenate([g0[...], g1[...], g2[...], g3[...]], axis=0)
        other[...] = dot(ph[:, CHUNK:], rows, 0, 0).astype(BF16)
        own[...] = dot(ph[:, :CHUNK], rows, 0, 0)

    cols = lambda rows: pl.BlockSpec((rows, WIDE), lambda i, seq: (0, i))
    return call(
        body,
        (4,),
        [full((4 * TOK, WIDE))] + [cols(TOK)] * 4,
        [cols(CHUNK)] * 2,
        [sds((CHUNK, 8 * CHUNK), F32), sds((CHUNK, 8 * CHUNK))],
        seq,
        (partner_hidden, *grads),
    )


def backward_half(seq, heads, grad_chunks, proj_rows, half):
    count = len(proj_rows)
    at = lambda j, seq: head_at(j + 2 * half, seq) & 1

    def body(seq_ref, *refs):
        chunks, weights = refs[12:16], refs[16 : 16 + 8 * count]
        dq_out, kv_own, kv_other, grad_att = refs[16 + 8 * count :]
        step = pl.program_id(0)

        @pl.when(step == 0)
        def _():
            total = None
            for d, chunk in enumerate(chunks):
                rows = jnp.concatenate(
                    [chunk[(r ^ d) * TOK : ((r ^ d) + 1) * TOK] for r in range(4)], axis=0
                )
                for h in range(2):
                    piece = rows[:, h * CHUNK : (h + 1) * CHUNK]
                    blocks = [weights[8 * w + 2 * d + h][...] for w in range(count)]
                    term = dot(piece, jnp.concatenate(blocks, axis=0), 1, 1)
                    total = term if total is None else total + term
            grad_att[0] = total[:, :HEAD].astype(BF16)
            grad_att[1] = total[:, HEAD:].astype(BF16)

        grad = grad_att[step]
        query, key, value = head_values(refs)
        raised = raised_scores(query, key)
        weight = raised * (1.0 / jnp.sum(raised, axis=-1, keepdims=True))
        grad_weight = dot(grad, value, 1, 1)
        row_dot = jnp.sum(weight * grad_weight, axis=-1, keepdims=True)
        d_scores = (weight * (grad_weight - row_dot)).astype(BF16)
        dq_out[...] = (dot(d_scores, key, 1, 0) * FACTOR).astype(BF16)
        d_key = (dot(d_scores, query, 0, 0) * FACTOR).astype(BF16)
        d_value = dot(weight.astype(BF16), grad, 0, 0).astype(BF16)
        rows = 4 * TOK
        kv_own[0] = d_key[:rows]
        kv_own[1] = d_value[:rows]
        kv_other[0] = d_key[rows:]
        kv_other[1] = d_value[rows:]

    pair = pl.BlockSpec((2, 4 * TOK, HEAD), lambda j, seq: (0, 0, at(j, seq)))
    return call(
        body,
        (2,),
        head_specs(2 * half)
        + [full((4 * TOK, WIDE))] * 4
        + [chunk_spec(weight.shape[0], rel) for weight in proj_rows for rel in range(8)],
        [pl.BlockSpec((4 * TOK, HEAD), lambda j, seq: (0, at(j, seq))), pair, pair],
        [sds((4 * TOK, CHUNK))] + [sds((2, 4 * TOK, CHUNK))] * 2,
        seq,
        (*heads, *grad_chunks, *[weight for weight in proj_rows for _ in range(8)]),
        scratch=[pltpu.VMEM((2, 4 * TOK, HEAD), BF16)],
    )


def add_key_grads(seq, own, other, query_grads):
    count = 2 + len(query_grads)

    def body(seq_ref, a, b, *refs):
        ins, outs = refs[: count - 2], refs[count - 2 :]
        for r, out in enumerate(outs):
            rows = slice(r * TOK, (r + 1) * TOK)
            for t in range(2):
                out[t] = (a[t, rows].astype(F32) + b[t, rows].astype(F32)).astype(BF16)
            for t, ref in enumerate(ins):
                out[2 + t] = ref[rows]

    return call(
        body,
        (1,),
        [full((2, 4 * TOK, CHUNK))] * 2 + [full((4 * TOK, CHUNK))] * (count - 2),
        [full((count, TOK, CHUNK))] * 4,
        [sds((count, TOK, CHUNK))] * 4,
        seq,
        (own, other, *query_grads),
    )


def exchange(pieces):
    got = [pieces[0], None, None, None]
    for r in (2, 1, 3):
        got[r] = seq_shift(pieces[r], 2 * r)
    return got


def half_block(array, lead):
    return (array, pl.BlockSpec((None, TOK, CHUNK), lambda i, seq: (lead, 0, 0)))


def steps(queries, key_vecs, value_vecs, hidden_in, out_proj, couple_proj, grad_mixed):
    odd_rep = lax.axis_index("rep").astype(jnp.int32) & 1
    seq = jnp.stack([lax.axis_index("seq").astype(jnp.int32), odd_rep])
    proj_half = rep_shift(half_rows(out_proj[0], odd_rep), 1)
    couple_half = rep_shift(half_rows(couple_proj[0], odd_rep), 1)
    pairs = relative_columns(seq, (key_vecs[0], value_vecs[0]))
    pairs = exchange(pairs)
    others = [seq_shift(pairs[r], 1) for r in range(4)]
    items = exchange(relative_columns(seq, (queries[0],)))
    grads = exchange([grad_mixed[0]] * 4)
    inputs = exchange(relative_columns(seq, (hidden_in[0],)))
    proj = (out_proj[0], proj_half, rep_shift(proj_half, 0))
    couple = (couple_proj[0], couple_half, rep_shift(couple_half, 0))
    heads = (*items, *pairs, *others)

    back = back_couple_product(seq, grads, couple)
    partner_back = branch_swap(back)
    chunk = grad_hidden_chunk(seq, grads, partner_back)
    chunks = exchange([chunk] * 4)

    sums = exchange(output_partial(seq, attend(seq, heads), proj))

    first = backward_half(seq, heads, chunks, proj[:1], 0)
    got_high = seq_shift(first[2], 1)
    second = backward_half(seq, heads, chunks, proj[1:], 1)
    got_low = seq_shift(second[2], 1)

    hidden = hidden_sum(seq, inputs, sums[0], sums[1:])
    partner_hidden = branch_swap(hidden)
    mixed_parts = exchange(mixed_partial(seq, partner_hidden, hidden, couple))
    couple_own, couple_other = couple_gradient(seq, partner_hidden, grads)
    couple_got = seq_shift(couple_other, 1)

    high = add_key_grads(seq, second[1], got_high, (first[0], second[0]))
    high = exchange(high)
    low = exchange(add_key_grads(seq, first[1], got_low, ()))

    def chunk_half(r, h):
        return (chunks[r], pl.BlockSpec((TOK, CHUNK), lambda i, seq: (r, h)))

    (grad_hid,) = absolute_columns(seq, [[(chunk_half(r, 0), chunk_half(r, 1))] for r in range(4)])
    mixed = mixed_parts[0]
    for part in mixed_parts[1:]:
        mixed = mixed + part.astype(F32)
    grad_cpl = couple_own + couple_got.astype(F32)
    grad_q, grad_k, grad_v = absolute_columns(
        seq,
        [
            [
                (half_block(high[r], 2), half_block(high[r], 3)),
                (half_block(low[r], 0), half_block(high[r], 0)),
                (half_block(low[r], 1), half_block(high[r], 1)),
            ]
            for r in range(4)
        ],
    )
    return (
        mixed.astype(BF16)[None],
        grad_hid[None],
        grad_q[None],
        grad_k[None],
        grad_v[None],
        grad_cpl[None],
    )


def solution(mesh):
    return jax.shard_map(
        steps,
        mesh=mesh,
        in_specs=(
            P("branch", ("rep", "seq"), None),
            P("branch", ("rep", "seq"), None),
            P("branch", ("rep", "seq"), None),
            P("branch", ("rep", "seq"), None),
            P("branch", "seq", None),
            P("branch", "seq", None),
            P("branch", ("rep", "seq"), None),
        ),
        out_specs=(
            P("branch", ("rep", "seq"), None),
            P("branch", ("rep", "seq"), None),
            P("branch", ("rep", "seq"), None),
            P("branch", ("rep", "seq"), None),
            P("branch", ("rep", "seq"), None),
            P("branch", "seq", "rep"),
        ),
        check_vma=False,
    )
```

```python
import math

import jax
import jax.numpy as jnp
from jax import lax
from jax.experimental import pallas as pl
from jax.experimental.pallas import tpu as pltpu
from jax.sharding import PartitionSpec as P


HEAD = 128
TOK = 128
CHUNK = 256
WIDE = 2 * CHUNK
FACTOR = 1.0 / math.sqrt(HEAD)
BF16 = jnp.bfloat16
F32 = jnp.float32
VMEM_LIMIT = 56 * 1024 * 1024


def seq_shift(value, mask):
    size = lax.axis_size("seq")
    return lax.ppermute(value, "seq", [(i, i ^ mask) for i in range(size)])


def branch_swap(value):
    return lax.ppermute(value, "branch", [(0, 1), (1, 0)])


def rep_shift(value, mask):
    seqs, reps = lax.axis_size("seq"), lax.axis_size("rep")
    pairs = [
        (s * reps + r, (s ^ mask) * reps + (r ^ 1)) for s in range(seqs) for r in range(reps)
    ]
    return lax.ppermute(value, ("seq", "rep"), pairs)


def half_rows(weight, odd_rep):
    return lax.dynamic_slice(weight, (HEAD * (1 - odd_rep), 0), (HEAD, weight.shape[1]))


def dot(left, right, left_dim, right_dim):
    return lax.dot_general(
        left, right, (((left_dim,), (right_dim,)), ((), ())), preferred_element_type=F32
    )


def full(shape):
    return pl.BlockSpec(shape, lambda *_: (0,) * len(shape))


def call(body, in_specs, out_blocks, out_shapes, place, args, scratch=()):
    specs = list(in_specs) + [full(arg.shape) for arg in args[len(in_specs) :]]
    return pl.pallas_call(
        body,
        out_shape=out_shapes,
        grid_spec=pltpu.PrefetchScalarGridSpec(
            num_scalar_prefetch=1,
            grid=(1,),
            in_specs=specs,
            out_specs=[full(block) for block in out_blocks],
            scratch_shapes=list(scratch),
        ),
        compiler_params=pltpu.CompilerParams(vmem_limit_bytes=VMEM_LIMIT),
    )(place, *args)


def sds(shape, dtype=BF16):
    return jax.ShapeDtypeStruct(shape, dtype)


def chunk(place, rel):
    return pl.ds(pl.multiple_of((place[0] ^ rel) * CHUNK, CHUNK), CHUNK)


def held_rows(place, mine, other, cols):
    first, second = mine[:, cols], other[:, cols]
    odd = place[1] == 1
    return jnp.concatenate(
        [jnp.where(odd, second, first), jnp.where(odd, first, second)], axis=0
    )


def stacked(refs):
    return jnp.concatenate([ref[...] for ref in refs], axis=0)


def block_rows(r):
    return slice(r * TOK, (r + 1) * TOK)


def relative_columns(place, arrays):
    count = len(arrays)

    def body(place_ref, *refs):
        ins, outs = refs[:count], refs[count:]
        for a in range(count):
            for rel in range(8):
                half = rel & 1
                outs[rel >> 1][a, :, half * CHUNK : (half + 1) * CHUNK] = ins[a][
                    :, chunk(place_ref, rel)
                ]

    shape = (count, TOK, WIDE)
    return call(body, [], [shape] * 4, [sds(shape)] * 4, place, arrays)


def back_couple_product(place, grads, couple):
    def body(place_ref, g0, g1, g2, g3, own, mine, other, out, picked):
        rows = stacked((g0, g1, g2, g3))
        held = held_rows(place_ref, mine, other, slice(None))
        out[:, :CHUNK] = dot(rows, own[...], 1, 1).astype(BF16)
        out[:, CHUNK:] = dot(rows, held, 1, 1).astype(BF16)
        for r, ref in enumerate((g0, g1, g2, g3)):
            picked[block_rows(r), :CHUNK] = ref[:, chunk(place_ref, 0)]
            picked[block_rows(r), CHUNK:] = ref[:, chunk(place_ref, 1)]

    shape = (4 * TOK, WIDE)
    return call(body, [], [shape] * 2, [sds(shape)] * 2, place, (*grads, *couple))


def head_values(refs, own, other):
    query = jnp.concatenate([ref[0, :, own] for ref in refs[:4]], axis=0)
    cols = [own] * 4 + [other] * 4
    key = jnp.concatenate([ref[0, :, c] for ref, c in zip(refs[4:12], cols)], axis=0)
    value = jnp.concatenate([ref[1, :, c] for ref, c in zip(refs[4:12], cols)], axis=0)
    return query, key, value


def raised_scores(query, key):
    scores = dot(query, key, 1, 1)
    base = FACTOR * math.log2(math.e)
    return jnp.exp2(scores * base - jnp.max(scores, axis=-1, keepdims=True) * base)


def head_cols(j):
    return pl.ds(pl.multiple_of(j * HEAD, HEAD), HEAD)


def forward_partial(place, heads, inputs, proj):
    def body(place_ref, *refs):
        own_in, (own_w, mine, other), outs = refs[12:16], refs[16:19], refs[19:23]
        attended = refs[23]

        def two_heads(half, carry):
            for h in range(2):
                cols = head_cols(2 * half + h)
                query, key, value = head_values(refs, cols, head_cols(2 * (1 - half) + h))
                raised = raised_scores(query, key)
                total = jnp.sum(raised, axis=-1, keepdims=True)
                result = dot(raised.astype(BF16), value, 1, 0) / total
                attended[:, cols] = result.astype(BF16)
            return carry

        lax.fori_loop(0, 2, two_heads, 0)
        first, second = attended[:, :CHUNK], attended[:, CHUNK:]
        for rel in range(8):
            dest, half = rel >> 1, rel & 1
            cols = chunk(place_ref, rel)
            part = dot(first, own_w[:, cols], 1, 0)
            part = part + dot(second, held_rows(place_ref, mine, other, cols), 1, 0)
            at = slice(half * CHUNK, (half + 1) * CHUNK)
            for r in range(4):
                block = part[block_rows(r)]
                if dest == 0:
                    block = block + own_in[r][0, :, at].astype(F32)
                outs[dest][block_rows(r ^ dest), at] = block.astype(outs[dest].dtype)

    shape = (4 * TOK, WIDE)
    return call(
        body,
        [],
        [shape] * 4,
        [sds(shape, F32)] + [sds(shape)] * 3,
        place,
        (*heads, *inputs, *proj),
        scratch=[pltpu.VMEM(shape, BF16)],
    )


def mixed_partial(place, partner_hidden, hidden, couple):
    def body(place_ref, other_hid, own_hid, own_w, mine, other, *outs):
        first, second = other_hid[:, :CHUNK], other_hid[:, CHUNK:]
        for rel in range(8):
            cols = chunk(place_ref, rel)
            part = dot(first, own_w[:, cols], 1, 0)
            part = part + dot(second, held_rows(place_ref, mine, other, cols), 1, 0)
            if rel < 2:
                part = part + own_hid[:, rel * CHUNK : (rel + 1) * CHUNK].astype(F32)
            for r in range(4):
                outs[r][:, cols] = part[block_rows(r)].astype(outs[r].dtype)

    shape = (TOK, 8 * CHUNK)
    return call(
        body,
        [],
        [shape] * 4,
        [sds(shape, F32)] + [sds(shape)] * 3,
        place,
        (partner_hidden, hidden, *couple),
    )


def couple_gradient(place, partner_hidden, grads):
    def body(place_ref, hid, g0, g1, g2, g3, own, other):
        rows = stacked((g0, g1, g2, g3))
        other[...] = dot(hid[:, CHUNK:], rows, 0, 0).astype(BF16)
        own[...] = dot(hid[:, :CHUNK], rows, 0, 0)

    shape = (CHUNK, 8 * CHUNK)
    return call(
        body,
        [],
        [shape] * 2,
        [sds(shape, F32), sds(shape)],
        place,
        (partner_hidden, *grads),
    )


def backward_half(place, heads, grad_chunks, proj_rows, half):
    count = len(proj_rows)

    def body(place_ref, *refs):
        chunks, weights = refs[12:16], refs[16 : 16 + count]
        dq_out, kv_own, kv_other, grads = refs[16 + count :]
        grad_att = None
        for d, ref in enumerate(chunks):
            rows = jnp.concatenate([ref[block_rows(r ^ d)] for r in range(4)], axis=0)
            for h in range(2):
                cols = chunk(place_ref, 2 * d + h)
                if count == 1:
                    weight = weights[0][:, cols]
                else:
                    weight = held_rows(place_ref, *weights, cols)
                term = dot(rows[:, h * CHUNK : (h + 1) * CHUNK], weight, 1, 1)
                grad_att = term if grad_att is None else grad_att + term
        grads[...] = grad_att.astype(BF16)
        rows = 4 * TOK

        def one_head(j, carry):
            cols = head_cols(j)
            grad = grads[:, cols]
            query, key, value = head_values(refs, cols, cols)
            raised = raised_scores(query, key)
            weight = raised * (1.0 / jnp.sum(raised, axis=-1, keepdims=True))
            grad_weight = dot(grad, value, 1, 1)
            row_dot = jnp.sum(weight * grad_weight, axis=-1, keepdims=True)
            d_scores = (weight * (grad_weight - row_dot)).astype(BF16)
            dq_out[:, cols] = (dot(d_scores, key, 1, 0) * FACTOR).astype(BF16)
            d_key = (dot(d_scores, query, 0, 0) * FACTOR).astype(BF16)
            d_value = dot(weight.astype(BF16), grad, 0, 0).astype(BF16)
            kv_own[0, :, cols] = d_key[:rows]
            kv_own[1, :, cols] = d_value[:rows]
            kv_other[0, :, cols] = d_key[rows:]
            kv_other[1, :, cols] = d_value[rows:]
            return carry

        lax.fori_loop(0, 2, one_head, 0)

    def side(lead, at):
        return pl.BlockSpec((lead, TOK, CHUNK), lambda i, place: (0, 0, at))

    specs = [side(1, half)] * 4 + [side(2, half)] * 4 + [side(2, 1 - half)] * 4
    pair = (2, 4 * TOK, CHUNK)
    return call(
        body,
        specs,
        [(4 * TOK, CHUNK), pair, pair],
        [sds((4 * TOK, CHUNK)), sds(pair), sds(pair)],
        place,
        (*heads, *grad_chunks, *proj_rows),
        scratch=[pltpu.VMEM((4 * TOK, CHUNK), BF16)],
    )


def add_key_grads(place, own, other, query_grads):
    count = 2 + len(query_grads)

    def body(place_ref, a, b, *refs):
        ins, outs = refs[: count - 2], refs[count - 2 :]
        for r, out in enumerate(outs):
            rows = block_rows(r)
            for t in range(2):
                out[t] = (a[t, rows].astype(F32) + b[t, rows].astype(F32)).astype(BF16)
            for t, ref in enumerate(ins):
                out[2 + t] = ref[rows]

    shape = (count, TOK, CHUNK)
    return call(
        body, [], [shape] * 4, [sds(shape)] * 4, place, (own, other, *query_grads)
    )


def gradient_columns(place, low, high):
    def body(place_ref, *refs):
        lows, highs, (q_out, k_out, v_out) = refs[:4], refs[4:8], refs[8:]
        for r in range(4):
            even, odd = chunk(place_ref, 2 * r), chunk(place_ref, 2 * r + 1)
            q_out[:, even] = highs[r][2]
            q_out[:, odd] = highs[r][3]
            k_out[:, even] = lows[r][0]
            k_out[:, odd] = highs[r][0]
            v_out[:, even] = lows[r][1]
            v_out[:, odd] = highs[r][1]

    shape = (TOK, 8 * CHUNK)
    return call(body, [], [shape] * 3, [sds(shape)] * 3, place, (*low, *high))


def grad_hidden_columns(place, chunks):
    def body(place_ref, c0, c1, c2, c3, out):
        for r, ref in enumerate((c0, c1, c2, c3)):
            out[:, chunk(place_ref, 2 * r)] = ref[:, :CHUNK]
            out[:, chunk(place_ref, 2 * r + 1)] = ref[:, CHUNK:]

    specs = [pl.BlockSpec((TOK, WIDE), lambda i, place, r=r: (r, 0)) for r in range(4)]
    shape = (TOK, 8 * CHUNK)
    return call(body, specs, [shape], [sds(shape)], place, chunks)[0]


def exchange(pieces):
    got = [pieces[0], None, None, None]
    for r in (2, 1, 3):
        got[r] = seq_shift(pieces[r], 2 * r)
    return got


def steps(queries, key_vecs, value_vecs, hidden_in, out_proj, couple_proj, grad_mixed):
    odd_rep = lax.axis_index("rep").astype(jnp.int32) & 1
    place = jnp.stack([lax.axis_index("seq").astype(jnp.int32), odd_rep])
    pairs = relative_columns(place, (key_vecs[0], value_vecs[0]))
    pairs = exchange(pairs)
    others = [seq_shift(pairs[r], 1) for r in range(4)]
    couple_half = rep_shift(half_rows(couple_proj[0], odd_rep), 1)
    proj_half = rep_shift(half_rows(out_proj[0], odd_rep), 1)
    grads = exchange([grad_mixed[0]] * 4)
    items = exchange(relative_columns(place, (queries[0],)))
    inputs = exchange(relative_columns(place, (hidden_in[0],)))
    couple = (couple_proj[0], couple_half, rep_shift(couple_half, 0))
    proj = (out_proj[0], proj_half, rep_shift(proj_half, 0))
    heads = (*items, *pairs, *others)

    back, picked = back_couple_product(place, grads, couple)
    partner_back = branch_swap(back)
    total = (picked.astype(F32) + partner_back.astype(F32)).astype(BF16)
    chunks = exchange([total] * 4)

    sums = exchange(forward_partial(place, heads, inputs, proj))

    first = backward_half(place, heads, chunks, proj[:1], 0)
    got_high = seq_shift(first[2], 1)
    second = backward_half(place, heads, chunks, proj[1:], 1)
    got_low = seq_shift(second[2], 1)

    hidden = sums[0]
    for part in sums[1:]:
        hidden = hidden + part.astype(F32)
    hidden = hidden.astype(BF16)
    partner_hidden = branch_swap(hidden)
    mixed_parts = exchange(mixed_partial(place, partner_hidden, hidden, couple))
    couple_own, couple_other = couple_gradient(place, partner_hidden, grads)
    couple_got = seq_shift(couple_other, 1)

    high = add_key_grads(place, second[1], got_high, (first[0], second[0]))
    high = exchange(high)
    low = exchange(add_key_grads(place, first[1], got_low, ()))

    grad_hid = grad_hidden_columns(place, chunks)
    mixed = mixed_parts[0]
    for part in mixed_parts[1:]:
        mixed = mixed + part.astype(F32)
    grad_cpl = couple_own + couple_got.astype(F32)
    grad_q, grad_k, grad_v = gradient_columns(place, low, high)
    return (
        mixed.astype(BF16)[None],
        grad_hid[None],
        grad_q[None],
        grad_k[None],
        grad_v[None],
        grad_cpl[None],
    )


def solution(mesh):
    return jax.shard_map(
        steps,
        mesh=mesh,
        in_specs=(
            P("branch", ("rep", "seq"), None),
            P("branch", ("rep", "seq"), None),
            P("branch", ("rep", "seq"), None),
            P("branch", ("rep", "seq"), None),
            P("branch", "seq", None),
            P("branch", "seq", None),
            P("branch", ("rep", "seq"), None),
        ),
        out_specs=(
            P("branch", ("rep", "seq"), None),
            P("branch", ("rep", "seq"), None),
            P("branch", ("rep", "seq"), None),
            P("branch", ("rep", "seq"), None),
            P("branch", ("rep", "seq"), None),
            P("branch", "seq", "rep"),
        ),
        check_vma=False,
    )
```

```python
import math

import jax
import jax.numpy as jnp
from jax import lax
from jax.experimental import pallas as pl
from jax.experimental.pallas import tpu as pltpu
from jax.sharding import PartitionSpec as P


HEAD = 128
TOK = 128
CHUNK = 256
WIDE = 2 * CHUNK
FACTOR = 1.0 / math.sqrt(HEAD)
BF16 = jnp.bfloat16
F32 = jnp.float32
VMEM_LIMIT = 56 * 1024 * 1024


def seq_shift(value, mask):
    size = lax.axis_size("seq")
    return lax.ppermute(value, "seq", [(i, i ^ mask) for i in range(size)])


def branch_swap(value):
    return lax.ppermute(value, "branch", [(0, 1), (1, 0)])


def rep_shift(value, mask):
    seqs, reps = lax.axis_size("seq"), lax.axis_size("rep")
    pairs = [
        (s * reps + r, (s ^ mask) * reps + (r ^ 1)) for s in range(seqs) for r in range(reps)
    ]
    return lax.ppermute(value, ("seq", "rep"), pairs)


def half_rows(weight, odd_rep):
    return lax.dynamic_slice(weight, (HEAD * (1 - odd_rep), 0), (HEAD, weight.shape[1]))


def dot(left, right, left_dim, right_dim):
    return lax.dot_general(
        left, right, (((left_dim,), (right_dim,)), ((), ())), preferred_element_type=F32
    )


def full(shape):
    return pl.BlockSpec(shape, lambda *_: (0,) * len(shape))


def call(body, in_specs, out_blocks, out_shapes, place, args, scratch=()):
    specs = list(in_specs) + [full(arg.shape) for arg in args[len(in_specs) :]]
    return pl.pallas_call(
        body,
        out_shape=out_shapes,
        grid_spec=pltpu.PrefetchScalarGridSpec(
            num_scalar_prefetch=1,
            grid=(1,),
            in_specs=specs,
            out_specs=[full(block) for block in out_blocks],
            scratch_shapes=list(scratch),
        ),
        compiler_params=pltpu.CompilerParams(vmem_limit_bytes=VMEM_LIMIT),
    )(place, *args)


def sds(shape, dtype=BF16):
    return jax.ShapeDtypeStruct(shape, dtype)


def chunk(place, rel):
    return pl.ds(pl.multiple_of((place[0] ^ rel) * CHUNK, CHUNK), CHUNK)


def held_rows(place, mine, other, cols):
    first, second = mine[:, cols], other[:, cols]
    odd = place[1] == 1
    return jnp.concatenate(
        [jnp.where(odd, second, first), jnp.where(odd, first, second)], axis=0
    )


def stacked(refs):
    return jnp.concatenate([ref[...] for ref in refs], axis=0)


def block_rows(r):
    return slice(r * TOK, (r + 1) * TOK)


def relative_columns(place, arrays):
    count = len(arrays)

    def body(place_ref, *refs):
        ins, outs = refs[:count], refs[count:]
        for a in range(count):
            for rel in range(8):
                half = rel & 1
                outs[rel >> 1][a, :, half * CHUNK : (half + 1) * CHUNK] = ins[a][
                    :, chunk(place_ref, rel)
                ]

    shape = (count, TOK, WIDE)
    return call(body, [], [shape] * 4, [sds(shape)] * 4, place, arrays)


def back_couple_product(place, grads, couple):
    def body(place_ref, g0, g1, g2, g3, own, mine, other, out, picked):
        rows = stacked((g0, g1, g2, g3))
        held = held_rows(place_ref, mine, other, slice(None))
        out[:, :CHUNK] = dot(rows, own[...], 1, 1).astype(BF16)
        out[:, CHUNK:] = dot(rows, held, 1, 1).astype(BF16)
        for r, ref in enumerate((g0, g1, g2, g3)):
            picked[block_rows(r), :CHUNK] = ref[:, chunk(place_ref, 0)]
            picked[block_rows(r), CHUNK:] = ref[:, chunk(place_ref, 1)]

    shape = (4 * TOK, WIDE)
    return call(body, [], [shape] * 2, [sds(shape)] * 2, place, (*grads, *couple))


def head_values(refs, own, other):
    query = jnp.concatenate([ref[0, :, own] for ref in refs[:4]], axis=0)
    cols = [own] * 4 + [other] * 4
    key = jnp.concatenate([ref[0, :, c] for ref, c in zip(refs[4:12], cols)], axis=0)
    value = jnp.concatenate([ref[1, :, c] for ref, c in zip(refs[4:12], cols)], axis=0)
    return query, key, value


def raised_scores(query, key):
    scores = dot(query, key, 1, 1)
    base = FACTOR * math.log2(math.e)
    return jnp.exp2(scores * base - jnp.max(scores, axis=-1, keepdims=True) * base)


def head_cols(j):
    return pl.ds(pl.multiple_of(j * HEAD, HEAD), HEAD)


def forward_partial(place, heads, proj):
    def body(place_ref, *refs):
        (own_w, mine, other), outs, attended = refs[12:15], refs[15:19], refs[19]

        def two_heads(half, carry):
            for h in range(2):
                cols = head_cols(2 * half + h)
                query, key, value = head_values(refs, cols, head_cols(2 * (1 - half) + h))
                raised = raised_scores(query, key)
                total = jnp.sum(raised, axis=-1, keepdims=True)
                result = dot(raised.astype(BF16), value, 1, 0) / total
                attended[:, cols] = result.astype(BF16)
            return carry

        lax.fori_loop(0, 2, two_heads, 0)
        first, second = attended[:, :CHUNK], attended[:, CHUNK:]
        for rel in range(8):
            dest, half = rel >> 1, rel & 1
            cols = chunk(place_ref, rel)
            part = dot(first, own_w[:, cols], 1, 0)
            part = part + dot(second, held_rows(place_ref, mine, other, cols), 1, 0)
            at = slice(half * CHUNK, (half + 1) * CHUNK)
            for r in range(4):
                block = part[block_rows(r)].astype(outs[dest].dtype)
                outs[dest][block_rows(r ^ dest), at] = block

    shape = (4 * TOK, WIDE)
    return call(
        body,
        [],
        [shape] * 4,
        [sds(shape, F32)] + [sds(shape)] * 3,
        place,
        (*heads, *proj),
        scratch=[pltpu.VMEM(shape, BF16)],
    )


def mixed_partial(place, partner_hidden, hidden, couple):
    def body(place_ref, other_hid, own_hid, own_w, mine, other, *outs):
        first, second = other_hid[:, :CHUNK], other_hid[:, CHUNK:]
        for rel in range(8):
            cols = chunk(place_ref, rel)
            part = dot(first, own_w[:, cols], 1, 0)
            part = part + dot(second, held_rows(place_ref, mine, other, cols), 1, 0)
            if rel < 2:
                part = part + own_hid[:, rel * CHUNK : (rel + 1) * CHUNK].astype(F32)
            for r in range(4):
                outs[r][:, cols] = part[block_rows(r)].astype(outs[r].dtype)

    shape = (TOK, 8 * CHUNK)
    return call(
        body,
        [],
        [shape] * 4,
        [sds(shape, F32)] + [sds(shape)] * 3,
        place,
        (partner_hidden, hidden, *couple),
    )


def couple_gradient(place, partner_hidden, grads):
    def body(place_ref, hid, g0, g1, g2, g3, own, other):
        rows = stacked((g0, g1, g2, g3))
        other[...] = dot(hid[:, CHUNK:], rows, 0, 0).astype(BF16)
        own[...] = dot(hid[:, :CHUNK], rows, 0, 0)

    shape = (CHUNK, 8 * CHUNK)
    return call(
        body,
        [],
        [shape] * 2,
        [sds(shape, F32), sds(shape)],
        place,
        (partner_hidden, *grads),
    )


def backward_half(place, heads, grad_chunks, proj_rows, half):
    count = len(proj_rows)

    def body(place_ref, *refs):
        chunks, weights = refs[12:16], refs[16 : 16 + count]
        dq_out, kv_own, kv_other, grads = refs[16 + count :]
        grad_att = None
        for d, ref in enumerate(chunks):
            rows = jnp.concatenate([ref[block_rows(r ^ d)] for r in range(4)], axis=0)
            for h in range(2):
                cols = chunk(place_ref, 2 * d + h)
                if count == 1:
                    weight = weights[0][:, cols]
                else:
                    weight = held_rows(place_ref, *weights, cols)
                term = dot(rows[:, h * CHUNK : (h + 1) * CHUNK], weight, 1, 1)
                grad_att = term if grad_att is None else grad_att + term
        grads[...] = grad_att.astype(BF16)
        rows = 4 * TOK

        def one_head(j, carry):
            cols = head_cols(j)
            grad = grads[:, cols]
            query, key, value = head_values(refs, cols, cols)
            raised = raised_scores(query, key)
            weight = raised * (1.0 / jnp.sum(raised, axis=-1, keepdims=True))
            grad_weight = dot(grad, value, 1, 1)
            row_dot = jnp.sum(weight * grad_weight, axis=-1, keepdims=True)
            d_scores = (weight * (grad_weight - row_dot)).astype(BF16)
            dq_out[:, cols] = (dot(d_scores, key, 1, 0) * FACTOR).astype(BF16)
            d_key = (dot(d_scores, query, 0, 0) * FACTOR).astype(BF16)
            d_value = dot(weight.astype(BF16), grad, 0, 0).astype(BF16)
            kv_own[0, :, cols] = d_key[:rows]
            kv_own[1, :, cols] = d_value[:rows]
            kv_other[0, :, cols] = d_key[rows:]
            kv_other[1, :, cols] = d_value[rows:]
            return carry

        lax.fori_loop(0, 2, one_head, 0)

    def side(lead, at):
        return pl.BlockSpec((lead, TOK, CHUNK), lambda i, place: (0, 0, at))

    specs = [side(1, half)] * 4 + [side(2, half)] * 4 + [side(2, 1 - half)] * 4
    pair = (2, 4 * TOK, CHUNK)
    return call(
        body,
        specs,
        [(4 * TOK, CHUNK), pair, pair],
        [sds((4 * TOK, CHUNK)), sds(pair), sds(pair)],
        place,
        (*heads, *grad_chunks, *proj_rows),
        scratch=[pltpu.VMEM((4 * TOK, CHUNK), BF16)],
    )


def add_key_grads(place, own, other, query_grads):
    count = 2 + len(query_grads)

    def body(place_ref, a, b, *refs):
        ins, outs = refs[: count - 2], refs[count - 2 :]
        for r, out in enumerate(outs):
            rows = block_rows(r)
            for t in range(2):
                out[t] = (a[t, rows].astype(F32) + b[t, rows].astype(F32)).astype(BF16)
            for t, ref in enumerate(ins):
                out[2 + t] = ref[rows]

    shape = (count, TOK, CHUNK)
    return call(
        body, [], [shape] * 4, [sds(shape)] * 4, place, (own, other, *query_grads)
    )


def gradient_columns(place, low, high):
    def body(place_ref, *refs):
        lows, highs, (q_out, k_out, v_out) = refs[:4], refs[4:8], refs[8:]
        for r in range(4):
            even, odd = chunk(place_ref, 2 * r), chunk(place_ref, 2 * r + 1)
            q_out[:, even] = highs[r][2]
            q_out[:, odd] = highs[r][3]
            k_out[:, even] = lows[r][0]
            k_out[:, odd] = highs[r][0]
            v_out[:, even] = lows[r][1]
            v_out[:, odd] = highs[r][1]

    shape = (TOK, 8 * CHUNK)
    return call(body, [], [shape] * 3, [sds(shape)] * 3, place, (*low, *high))


def grad_hidden_columns(place, chunks):
    def body(place_ref, c0, c1, c2, c3, out):
        for r, ref in enumerate((c0, c1, c2, c3)):
            out[:, chunk(place_ref, 2 * r)] = ref[:, :CHUNK]
            out[:, chunk(place_ref, 2 * r + 1)] = ref[:, CHUNK:]

    specs = [pl.BlockSpec((TOK, WIDE), lambda i, place, r=r: (r, 0)) for r in range(4)]
    shape = (TOK, 8 * CHUNK)
    return call(body, specs, [shape], [sds(shape)], place, chunks)[0]


def exchange(pieces):
    got = [pieces[0], None, None, None]
    for r in (2, 1, 3):
        got[r] = seq_shift(pieces[r], 2 * r)
    return got


def steps(queries, key_vecs, value_vecs, hidden_in, out_proj, couple_proj, grad_mixed):
    odd_rep = lax.axis_index("rep").astype(jnp.int32) & 1
    place = jnp.stack([lax.axis_index("seq").astype(jnp.int32), odd_rep])
    pairs = relative_columns(place, (key_vecs[0], value_vecs[0]))
    pairs = exchange(pairs)
    others = [seq_shift(pairs[r], 1) for r in range(4)]
    couple_half = rep_shift(half_rows(couple_proj[0], odd_rep), 1)
    proj_half = rep_shift(half_rows(out_proj[0], odd_rep), 1)
    grads = exchange([grad_mixed[0]] * 4)
    items = exchange(relative_columns(place, (queries[0],)))
    inputs = exchange(relative_columns(place, (hidden_in[0],)))
    couple = (couple_proj[0], couple_half, rep_shift(couple_half, 0))
    proj = (out_proj[0], proj_half, rep_shift(proj_half, 0))
    heads = (*items, *pairs, *others)

    back, picked = back_couple_product(place, grads, couple)
    partner_back = branch_swap(back)
    total = (picked.astype(F32) + partner_back.astype(F32)).astype(BF16)
    chunks = exchange([total] * 4)

    sums = exchange(forward_partial(place, heads, proj))

    first = backward_half(place, heads, chunks, proj[:1], 0)
    got_high = seq_shift(first[2], 1)
    second = backward_half(place, heads, chunks, proj[1:], 1)
    got_low = seq_shift(second[2], 1)

    hidden = sums[0] + jnp.concatenate([block[0] for block in inputs]).astype(F32)
    for part in sums[1:]:
        hidden = hidden + part.astype(F32)
    hidden = hidden.astype(BF16)
    partner_hidden = branch_swap(hidden)
    mixed_parts = exchange(mixed_partial(place, partner_hidden, hidden, couple))
    couple_own, couple_other = couple_gradient(place, partner_hidden, grads)
    couple_got = seq_shift(couple_other, 1)

    high = add_key_grads(place, second[1], got_high, (first[0], second[0]))
    high = exchange(high)
    low = exchange(add_key_grads(place, first[1], got_low, ()))

    grad_hid = grad_hidden_columns(place, chunks)
    mixed = mixed_parts[0]
    for part in mixed_parts[1:]:
        mixed = mixed + part.astype(F32)
    grad_cpl = couple_own + couple_got.astype(F32)
    grad_q, grad_k, grad_v = gradient_columns(place, low, high)
    return (
        mixed.astype(BF16)[None],
        grad_hid[None],
        grad_q[None],
        grad_k[None],
        grad_v[None],
        grad_cpl[None],
    )


def solution(mesh):
    return jax.shard_map(
        steps,
        mesh=mesh,
        in_specs=(
            P("branch", ("rep", "seq"), None),
            P("branch", ("rep", "seq"), None),
            P("branch", ("rep", "seq"), None),
            P("branch", ("rep", "seq"), None),
            P("branch", "seq", None),
            P("branch", "seq", None),
            P("branch", ("rep", "seq"), None),
        ),
        out_specs=(
            P("branch", ("rep", "seq"), None),
            P("branch", ("rep", "seq"), None),
            P("branch", ("rep", "seq"), None),
            P("branch", ("rep", "seq"), None),
            P("branch", ("rep", "seq"), None),
            P("branch", "seq", "rep"),
        ),
        check_vma=False,
    )
```

```python
import math

import jax
import jax.numpy as jnp
from jax import lax
from jax.experimental import pallas as pl
from jax.experimental.pallas import tpu as pltpu
from jax.sharding import PartitionSpec as P


HEAD = 128
TOK = 128
CHUNK = 256
WIDE = 2 * CHUNK
FACTOR = 1.0 / math.sqrt(HEAD)
BF16 = jnp.bfloat16
F32 = jnp.float32
VMEM_LIMIT = 56 * 1024 * 1024


def seq_shift(value, mask):
    size = lax.axis_size("seq")
    return lax.ppermute(value, "seq", [(i, i ^ mask) for i in range(size)])


def branch_swap(value):
    return lax.ppermute(value, "branch", [(0, 1), (1, 0)])


def rep_shift(value, mask):
    seqs, reps = lax.axis_size("seq"), lax.axis_size("rep")
    pairs = [
        (s * reps + r, (s ^ mask) * reps + (r ^ 1)) for s in range(seqs) for r in range(reps)
    ]
    return lax.ppermute(value, ("seq", "rep"), pairs)


def half_rows(weight, odd_rep):
    return lax.dynamic_slice(weight, (HEAD * (1 - odd_rep), 0), (HEAD, weight.shape[1]))


def dot(left, right, left_dim, right_dim):
    return lax.dot_general(
        left, right, (((left_dim,), (right_dim,)), ((), ())), preferred_element_type=F32
    )


def full(shape):
    return pl.BlockSpec(shape, lambda *_: (0,) * len(shape))


def call(body, in_specs, out_blocks, out_shapes, place, args, scratch=()):
    specs = list(in_specs) + [full(arg.shape) for arg in args[len(in_specs) :]]
    return pl.pallas_call(
        body,
        out_shape=out_shapes,
        grid_spec=pltpu.PrefetchScalarGridSpec(
            num_scalar_prefetch=1,
            grid=(1,),
            in_specs=specs,
            out_specs=[full(block) for block in out_blocks],
            scratch_shapes=list(scratch),
        ),
        compiler_params=pltpu.CompilerParams(vmem_limit_bytes=VMEM_LIMIT),
    )(place, *args)


def sds(shape, dtype=BF16):
    return jax.ShapeDtypeStruct(shape, dtype)


def chunk(place, rel):
    return pl.ds(pl.multiple_of((place[0] ^ rel) * CHUNK, CHUNK), CHUNK)


def held_rows(place, mine, other, cols):
    first, second = mine[:, cols], other[:, cols]
    odd = place[1] == 1
    return jnp.concatenate(
        [jnp.where(odd, second, first), jnp.where(odd, first, second)], axis=0
    )


def stacked(refs):
    return jnp.concatenate([ref[...] for ref in refs], axis=0)


def block_rows(r):
    return slice(r * TOK, (r + 1) * TOK)


def relative_columns(place, arrays):
    count = len(arrays)

    def body(place_ref, *refs):
        ins, outs = refs[:count], refs[count:]
        for a in range(count):
            for rel in range(8):
                half = rel & 1
                outs[rel >> 1][a, :, half * CHUNK : (half + 1) * CHUNK] = ins[a][
                    :, chunk(place_ref, rel)
                ]

    shape = (count, TOK, WIDE)
    return call(body, [], [shape] * 4, [sds(shape)] * 4, place, arrays)


def back_couple_product(place, grads, couple):
    def body(place_ref, g0, g1, g2, g3, own, mine, other, out, picked):
        rows = stacked((g0, g1, g2, g3))
        held = held_rows(place_ref, mine, other, slice(None))
        out[:, :CHUNK] = dot(rows, own[...], 1, 1).astype(BF16)
        out[:, CHUNK:] = dot(rows, held, 1, 1).astype(BF16)
        for r, ref in enumerate((g0, g1, g2, g3)):
            picked[block_rows(r), :CHUNK] = ref[:, chunk(place_ref, 0)]
            picked[block_rows(r), CHUNK:] = ref[:, chunk(place_ref, 1)]

    shape = (4 * TOK, WIDE)
    return call(body, [], [shape] * 2, [sds(shape)] * 2, place, (*grads, *couple))


def head_values(refs, own, other):
    query = jnp.concatenate([ref[0, :, own] for ref in refs[:4]], axis=0)
    cols = [own] * 4 + [other] * 4
    key = jnp.concatenate([ref[0, :, c] for ref, c in zip(refs[4:12], cols)], axis=0)
    value = jnp.concatenate([ref[1, :, c] for ref, c in zip(refs[4:12], cols)], axis=0)
    return query, key, value


def raised_scores(query, key):
    scores = dot(query, key, 1, 1)
    base = FACTOR * math.log2(math.e)
    return jnp.exp2(scores * base - jnp.max(scores, axis=-1, keepdims=True) * base)


def head_cols(j):
    return pl.ds(pl.multiple_of(j * HEAD, HEAD), HEAD)


def forward_partial(place, heads, proj):
    def body(place_ref, *refs):
        (own_w, mine, other), outs, attended = refs[12:15], refs[15:19], refs[19]

        def two_heads(half, carry):
            for h in range(2):
                cols = head_cols(2 * half + h)
                query, key, value = head_values(refs, cols, head_cols(2 * (1 - half) + h))
                raised = raised_scores(query, key)
                total = jnp.sum(raised, axis=-1, keepdims=True)
                result = dot(raised.astype(BF16), value, 1, 0) / total
                attended[:, cols] = result.astype(BF16)
            return carry

        lax.fori_loop(0, 2, two_heads, 0)
        first, second = attended[:, :CHUNK], attended[:, CHUNK:]
        for rel in range(8):
            dest, half = rel >> 1, rel & 1
            cols = chunk(place_ref, rel)
            part = dot(first, own_w[:, cols], 1, 0)
            part = part + dot(second, held_rows(place_ref, mine, other, cols), 1, 0)
            at = slice(half * CHUNK, (half + 1) * CHUNK)
            for r in range(4):
                block = part[block_rows(r)].astype(outs[dest].dtype)
                outs[dest][block_rows(r ^ dest), at] = block

    shape = (4 * TOK, WIDE)
    return call(
        body,
        [],
        [shape] * 4,
        [sds(shape, F32)] + [sds(shape)] * 3,
        place,
        (*heads, *proj),
        scratch=[pltpu.VMEM(shape, BF16)],
    )


def mixed_partial(place, partner_hidden, hidden, couple):
    def body(place_ref, other_hid, own_hid, own_w, mine, other, *outs):
        first, second = other_hid[:, :CHUNK], other_hid[:, CHUNK:]
        for rel in range(8):
            cols = chunk(place_ref, rel)
            part = dot(first, own_w[:, cols], 1, 0)
            part = part + dot(second, held_rows(place_ref, mine, other, cols), 1, 0)
            if rel < 2:
                part = part + own_hid[:, rel * CHUNK : (rel + 1) * CHUNK].astype(F32)
            for r in range(4):
                outs[r][:, cols] = part[block_rows(r)].astype(outs[r].dtype)

    shape = (TOK, 8 * CHUNK)
    return call(
        body,
        [],
        [shape] * 4,
        [sds(shape, F32)] + [sds(shape)] * 3,
        place,
        (partner_hidden, hidden, *couple),
    )


def couple_gradient(place, partner_hidden, grads):
    def body(place_ref, hid, g0, g1, g2, g3, own, other):
        rows = stacked((g0, g1, g2, g3))
        other[...] = dot(hid[:, CHUNK:], rows, 0, 0).astype(BF16)
        own[...] = dot(hid[:, :CHUNK], rows, 0, 0)

    shape = (CHUNK, 8 * CHUNK)
    return call(
        body,
        [],
        [shape] * 2,
        [sds(shape, F32), sds(shape)],
        place,
        (partner_hidden, *grads),
    )


def backward_half(place, heads, grad_chunks, proj_rows, half):
    count = len(proj_rows)

    def body(place_ref, *refs):
        chunks, weights = refs[12:16], refs[16 : 16 + count]
        dq_out, kv_own, kv_other, grads = refs[16 + count :]
        grad_att = None
        for d, ref in enumerate(chunks):
            rows = jnp.concatenate([ref[block_rows(r ^ d)] for r in range(4)], axis=0)
            for h in range(2):
                cols = chunk(place_ref, 2 * d + h)
                if count == 1:
                    weight = weights[0][:, cols]
                else:
                    weight = held_rows(place_ref, *weights, cols)
                term = dot(rows[:, h * CHUNK : (h + 1) * CHUNK], weight, 1, 1)
                grad_att = term if grad_att is None else grad_att + term
        grads[...] = grad_att.astype(BF16)
        rows = 4 * TOK

        def one_head(j, carry):
            cols = head_cols(j)
            grad = grads[:, cols]
            query, key, value = head_values(refs, cols, cols)
            raised = raised_scores(query, key)
            weight = raised * (1.0 / jnp.sum(raised, axis=-1, keepdims=True))
            grad_weight = dot(grad, value, 1, 1)
            row_dot = jnp.sum(weight * grad_weight, axis=-1, keepdims=True)
            d_scores = (weight * (grad_weight - row_dot)).astype(BF16)
            dq_out[:, cols] = (dot(d_scores, key, 1, 0) * FACTOR).astype(BF16)
            d_key = (dot(d_scores, query, 0, 0) * FACTOR).astype(BF16)
            d_value = dot(weight.astype(BF16), grad, 0, 0).astype(BF16)
            kv_own[0, :, cols] = d_key[:rows]
            kv_own[1, :, cols] = d_value[:rows]
            kv_other[0, :, cols] = d_key[rows:]
            kv_other[1, :, cols] = d_value[rows:]
            return carry

        lax.fori_loop(0, 2, one_head, 0)

    def side(lead, at):
        return pl.BlockSpec((lead, TOK, CHUNK), lambda i, place: (0, 0, at))

    specs = [side(1, half)] * 4 + [side(2, half)] * 4 + [side(2, 1 - half)] * 4
    pair = (2, 4 * TOK, CHUNK)
    return call(
        body,
        specs,
        [(4 * TOK, CHUNK), pair, pair],
        [sds((4 * TOK, CHUNK)), sds(pair), sds(pair)],
        place,
        (*heads, *grad_chunks, *proj_rows),
        scratch=[pltpu.VMEM((4 * TOK, CHUNK), BF16)],
    )


def add_key_grads(place, own, other, query_grads):
    count = 2 + len(query_grads)

    def body(place_ref, a, b, *refs):
        ins, outs = refs[: count - 2], refs[count - 2 :]
        for r, out in enumerate(outs):
            rows = block_rows(r)
            for t in range(2):
                out[t] = (a[t, rows].astype(F32) + b[t, rows].astype(F32)).astype(BF16)
            for t, ref in enumerate(ins):
                out[2 + t] = ref[rows]

    shape = (count, TOK, CHUNK)
    return call(
        body, [], [shape] * 4, [sds(shape)] * 4, place, (own, other, *query_grads)
    )


def query_columns(place, high):
    def body(place_ref, h0, h1, h2, h3, out):
        for r, ref in enumerate((h0, h1, h2, h3)):
            out[:, chunk(place_ref, 2 * r)] = ref[2]
            out[:, chunk(place_ref, 2 * r + 1)] = ref[3]

    shape = (TOK, 8 * CHUNK)
    return call(body, [], [shape], [sds(shape)], place, high)[0]


def key_columns(place, low, high):
    def body(place_ref, *refs):
        lows, highs, outs = refs[:4], refs[4:8], refs[8:]
        for r in range(4):
            for t, out in enumerate(outs):
                out[:, chunk(place_ref, 2 * r)] = lows[r][t]
                out[:, chunk(place_ref, 2 * r + 1)] = highs[r][t]

    pair = pl.BlockSpec((2, TOK, CHUNK), lambda i, place: (0, 0, 0))
    shape = (TOK, 8 * CHUNK)
    args = (*low, *high)
    return call(body, [pair] * 8, [shape] * 2, [sds(shape)] * 2, place, args)


def grad_hidden_columns(place, chunks):
    def body(place_ref, c0, c1, c2, c3, out):
        for r, ref in enumerate((c0, c1, c2, c3)):
            out[:, chunk(place_ref, 2 * r)] = ref[:, :CHUNK]
            out[:, chunk(place_ref, 2 * r + 1)] = ref[:, CHUNK:]

    specs = [pl.BlockSpec((TOK, WIDE), lambda i, place, r=r: (r, 0)) for r in range(4)]
    shape = (TOK, 8 * CHUNK)
    return call(body, specs, [shape], [sds(shape)], place, chunks)[0]


def exchange(pieces):
    got = [pieces[0], None, None, None]
    for r in (2, 1, 3):
        got[r] = seq_shift(pieces[r], 2 * r)
    return got


def steps(queries, key_vecs, value_vecs, hidden_in, out_proj, couple_proj, grad_mixed):
    odd_rep = lax.axis_index("rep").astype(jnp.int32) & 1
    place = jnp.stack([lax.axis_index("seq").astype(jnp.int32), odd_rep])
    pairs = relative_columns(place, (key_vecs[0], value_vecs[0]))
    pairs = exchange(pairs)
    others = [seq_shift(pairs[r], 1) for r in range(4)]
    couple_sent = half_rows(couple_proj[0], odd_rep)
    couple_half = rep_shift(couple_sent, 1)
    proj_half = rep_shift(half_rows(out_proj[0], odd_rep), 1)
    grads = exchange([grad_mixed[0]] * 4)
    items = exchange(relative_columns(place, (queries[0],)))
    inputs = exchange(relative_columns(place, (hidden_in[0],)))
    couple = (couple_proj[0], couple_half, rep_shift(couple_half, 0))
    proj = (out_proj[0], proj_half, rep_shift(proj_half, 0))
    heads = (*items, *pairs, *others)

    back, picked = back_couple_product(place, grads, couple)
    partner_back = branch_swap(back)
    total = (picked.astype(F32) + partner_back.astype(F32)).astype(BF16)
    chunks = exchange([total] * 4)

    sums = exchange(forward_partial(place, heads, proj))

    first = backward_half(place, heads, chunks, proj[:1], 0)
    got_high = seq_shift(first[2], 1)
    second = backward_half(place, heads, chunks, proj[1:], 1)
    got_low = seq_shift(second[2], 1)

    hidden = sums[0] + jnp.concatenate([block[0] for block in inputs]).astype(F32)
    for part in sums[1:]:
        hidden = hidden + part.astype(F32)
    hidden = hidden.astype(BF16)
    partner_hidden = branch_swap(hidden)
    mixed_parts = exchange(mixed_partial(place, partner_hidden, hidden, couple))
    couple_own, couple_other = couple_gradient(place, partner_hidden, grads)
    couple_got = seq_shift(couple_other, 1)

    high = add_key_grads(place, second[1], got_high, (first[0], second[0]))
    high = exchange(high)
    low = exchange(add_key_grads(place, first[1], got_low, ()))

    grad_hid = grad_hidden_columns(place, chunks)
    mixed = mixed_parts[0]
    for part in mixed_parts[1:]:
        mixed = mixed + part.astype(F32)
    mixed = mixed.astype(BF16)[None]
    grad_cpl = couple_own + couple_got.astype(F32)
    grad_q = query_columns(place, high)
    grad_k, grad_v = key_columns(place, low, high)
    return (
        mixed,
        grad_hid[None],
        grad_q[None],
        grad_k[None],
        grad_v[None],
        grad_cpl[None],
    )


def solution(mesh):
    return jax.shard_map(
        steps,
        mesh=mesh,
        in_specs=(
            P("branch", ("rep", "seq"), None),
            P("branch", ("rep", "seq"), None),
            P("branch", ("rep", "seq"), None),
            P("branch", ("rep", "seq"), None),
            P("branch", "seq", None),
            P("branch", "seq", None),
            P("branch", ("rep", "seq"), None),
        ),
        out_specs=(
            P("branch", ("rep", "seq"), None),
            P("branch", ("rep", "seq"), None),
            P("branch", ("rep", "seq"), None),
            P("branch", ("rep", "seq"), None),
            P("branch", ("rep", "seq"), None),
            P("branch", "seq", "rep"),
        ),
        check_vma=False,
    )
```
